32 devices in a mesh: sec: 4 (over y, x), tile: 8 (over z, core).
Axes of the slice: x: 2, y: 2, z: 4, core: 2. Of those that a mesh axis runs over, the one named last changes fastest.
Arguments:
- pan_source: bfloat16 [32, 256, 384], P(('sec', 'tile'))
- ms_source: bfloat16 [8, 32, 64, 96], P(None, ('sec', 'tile'))
- row_tap: int32 [32, 256], P(('sec', 'tile')), may hold values from 0 to 316, as said below
- row_frac: float32 [32, 256], P(('sec', 'tile')), may hold values from 0 to 1
- col_tap: int32 [32, 384], P(('sec', 'tile')), may hold values from 0 to 444, as said below
- col_frac: float32 [32, 384], P(('sec', 'tile')), may hold values from 0 to 1
- ms_row_tap: int32 [32, 256], P(('sec', 'tile')), may hold values from 0 to 76, as said below
- ms_row_frac: float32 [32, 256], P(('sec', 'tile')), may hold values from 0 to 1
- ms_col_tap: int32 [32, 384], P(('sec', 'tile')), may hold values from 0 to 108, as said below
- ms_col_frac: float32 [32, 384], P(('sec', 'tile')), may hold values from 0 to 1
Outputs:
- ms_sharp: bfloat16 [8, 32, 256, 384], P(None, ('sec', 'tile'))
The draws below stay inside these ranges and needn't reach their ends.
Inputs may be any that keep to these rules, and one draw needn't show every extreme that they name: Each row of row_tap starts at 0 and rises by 0, 1 or 2 from one map row to the next. Each row of col_tap starts at 0 and rises by 0, 1 or 2 from one map column to the next. Each row of ms_row_tap starts at 0 and rises by 0 or 1 from one map row to the next. Each row of ms_col_tap starts at 0 and rises by 0 or 1 from one map column to the next.
All inputs are finite; a program needn't handle non-finite values.
Results may differ from the reference program's by a relative error of at most 0.0045.
Values may be sent and summed in bfloat16 or wider, within the bound.
A program may use at most 128 MiB of HBM per device.

```python
import math
import jax
import jax.numpy as jnp
from jax import lax

BANDS = 8
TR = 256
TC = 384
MR = 64
MC = 96
HALO = 32
MHALO = 8
RADIUS = 8
NT = 32


def sensor_fields(key):
    keys_all = jax.random.split(jax.random.fold_in(key, 5), 9)
    coarse = jnp.clip(jax.random.normal(keys_all[0], (NT, MR, MC), jnp.float32), -4.0, 4.0)
    fine = jnp.clip(jax.random.normal(keys_all[1], (NT, TR, TC), jnp.float32), -4.0, 4.0)
    ms_noise = jnp.clip(jax.random.normal(keys_all[2], (BANDS, NT, MR, MC), jnp.float32), -4.0, 4.0)
    bright_share = 1.0 / 12.0
    bright_low = 2.5
    bright_high = 4.0
    darker_low = 0.35
    darker_high = 1.0
    mixing = jax.random.uniform(keys_all[4], (BANDS, 1, 1, 1), jnp.float32, 0.3, 0.9)
    upsampled = jnp.repeat(jnp.repeat(coarse, 4, axis=1), 4, axis=2)
    pan = 0.6 * upsampled + 0.8 * fine
    row_scale = jnp.exp(jax.random.uniform(keys_all[5], (NT, TR, 1), jnp.float32, math.log(0.5), math.log(2.0)))
    column_keys = jax.random.split(keys_all[6], 3)
    chooser = jax.random.uniform(column_keys[0], (NT, 1, TC), jnp.float32, 0.0, 1.0)
    bright = jnp.exp(jax.random.uniform(column_keys[1], (NT, 1, TC), jnp.float32, math.log(bright_low), math.log(bright_high)))
    darker = jnp.exp(jax.random.uniform(column_keys[2], (NT, 1, TC), jnp.float32, math.log(darker_low), math.log(darker_high)))
    col_scale = jnp.where(chooser < bright_share, bright, darker)
    pan = pan * row_scale * col_scale
    bands = mixing * coarse[None] + jnp.sqrt(1.0 - mixing * mixing) * ms_noise
    ms_row_scale = jnp.exp(jax.random.uniform(keys_all[7], (1, NT, MR, 1), jnp.float32, math.log(0.5), math.log(2.0)))
    ms_col_scale = jnp.exp(jax.random.uniform(keys_all[8], (1, NT, 1, MC), jnp.float32, math.log(0.5), math.log(2.0)))
    bands = bands * ms_row_scale * ms_col_scale
    return (pan, bands)


def draw_pan_source(key, part):
    pan, bands = sensor_fields(key)
    return pan.astype(jnp.bfloat16)


def draw_ms_source(key, part):
    pan, bands = sensor_fields(key)
    return bands.astype(jnp.bfloat16)


def tap_table(key, count, length, margin):
    zeros_count = length // 8
    twos_count = 2 * margin - 3 + zeros_count
    keys_all = jax.random.split(key, count)

    def one_row(row_key):
        shuffled = jax.random.permutation(row_key, length - 1)
        increments = jnp.where(shuffled < zeros_count, 0, jnp.where(shuffled < zeros_count + twos_count, 2, 1)).astype(jnp.int32)
        return jnp.concatenate([jnp.zeros((1,), jnp.int32), jnp.cumsum(increments).astype(jnp.int32)])
    return jax.vmap(one_row)(keys_all)


def coarse_table(key, count, length, rise_total):
    keys_all = jax.random.split(key, count)

    def one_row(row_key):
        shuffled = jax.random.permutation(row_key, length - 1)
        increments = jnp.where(shuffled < rise_total, 1, 0).astype(jnp.int32)
        return jnp.concatenate([jnp.zeros((1,), jnp.int32), jnp.cumsum(increments).astype(jnp.int32)])
    return jax.vmap(one_row)(keys_all)


def draw_row_tap(key, part):
    return tap_table(jax.random.fold_in(key, 11), NT, TR, HALO)


def draw_col_tap(key, part):
    return tap_table(jax.random.fold_in(key, 23), NT, TC, HALO)


def draw_ms_row_tap(key, part):
    return coarse_table(jax.random.fold_in(key, 37), NT, TR, MR + 2 * MHALO - 4)


def draw_ms_col_tap(key, part):
    return coarse_table(jax.random.fold_in(key, 41), NT, TC, MC + 2 * MHALO - 4)


def block_levels(stream_key, dims, cuts, least, high):
    def one(position, blocks):
        draws = jax.random.uniform(jax.random.fold_in(jax.random.fold_in(stream_key, 6), position), (blocks,), jnp.float32, least / len(cuts), high / len(cuts))
        return jnp.repeat(jnp.exp(draws), dims[position] // blocks).reshape((-1,) + (1,) * (len(dims) - position - 1))

    loudness = one(*cuts[0])
    for cut in cuts[1:]:
        loudness = loudness * one(*cut)
    return loudness


def setup_inputs(seed: int = 0) -> dict:
    key_list = jax.random.split(jax.random.key(seed), 11)
    return {
        "pan_source": draw_pan_source(jax.random.fold_in(key_list[10], 71), 0),
        "ms_source": draw_ms_source(jax.random.fold_in(key_list[10], 71), 0),
        "row_tap": draw_row_tap(jax.random.fold_in(key_list[10], 71), 0),
        "row_frac": jnp.clip(1.0 * jax.random.uniform(key_list[3], (NT, TR), jnp.float32) ** block_levels(key_list[3], (NT, TR), ((0, 32),), -0.2, 0.2), 0.0, 1.0),
        "col_tap": draw_col_tap(jax.random.fold_in(key_list[10], 71), 0),
        "col_frac": jnp.clip(1.0 * jax.random.uniform(key_list[5], (NT, TC), jnp.float32) ** block_levels(key_list[5], (NT, TC), ((0, 32),), -0.2, 0.2), 0.0, 1.0),
        "ms_row_tap": draw_ms_row_tap(jax.random.fold_in(key_list[10], 71), 0),
        "ms_row_frac": jnp.clip(1.0 * jax.random.uniform(key_list[7], (NT, TR), jnp.float32) ** block_levels(key_list[7], (NT, TR), ((0, 32),), -0.2, 0.2), 0.0, 1.0),
        "ms_col_tap": draw_ms_col_tap(jax.random.fold_in(key_list[10], 71), 0),
        "ms_col_frac": jnp.clip(1.0 * jax.random.uniform(key_list[9], (NT, TC), jnp.float32) ** block_levels(key_list[9], (NT, TC), ((0, 32),), -0.2, 0.2), 0.0, 1.0),
    }


EPSILON = 0.1


def cubic_weights(fraction):
    linear = fraction.astype(jnp.float32)
    squared = linear * linear
    cubed = squared * linear
    return jnp.stack([-0.5 * cubed + squared - 0.5 * linear,
                      1.5 * cubed - 2.5 * squared + 1.0,
                      -1.5 * cubed + 2.0 * squared + 0.5 * linear,
                      0.5 * cubed - 0.5 * squared], axis=0)


def rounded(values):
    return lax.optimization_barrier(values.astype(jnp.bfloat16)).astype(jnp.float32)


def window_sum(values, along_axis, window):
    total_length = values.shape[along_axis]
    kept_length = total_length - window + 1
    result = None
    partial_value = values
    stride = 1
    begin_at = 0
    while stride <= window:
        if window & stride:
            addend = lax.slice_in_dim(partial_value, begin_at, begin_at + kept_length, axis=along_axis)
            result = addend if result is None else result + addend
            begin_at = begin_at + stride
        if stride * 2 <= window:
            extent = partial_value.shape[along_axis]
            partial_value = lax.slice_in_dim(partial_value, 0, extent - stride, axis=along_axis) + lax.slice_in_dim(partial_value, stride, extent, axis=along_axis)
        stride = stride * 2
    return result


def coverage(anchor, amount, extent, radius):
    places = anchor + lax.iota(jnp.int32, amount)
    highest = jnp.minimum(places + radius, extent - 1)
    lowest = jnp.maximum(places - radius, 0)
    return (highest - lowest + 1).astype(jnp.float32)


def resample_all(stack, first_rows, row_fracs, first_cols, col_fracs, margin, out_rows, out_cols):
    channels = stack.shape[0]
    tiles_all = stack.shape[1]
    tile_rows = stack.shape[2]
    tile_cols = stack.shape[3]
    grid_rows = tiles_all // 4
    sensor_map = stack.reshape(channels, grid_rows, 4, tile_rows, tile_cols).transpose(0, 1, 3, 2, 4).reshape(channels, grid_rows * tile_rows, 4 * tile_cols)
    padded = jnp.pad(sensor_map, ((0, 0), (margin, margin), (margin, margin)))

    def one_tile(tile):
        anchor_row = ((tile // 4) * tile_rows).astype(jnp.int32)
        anchor_col = ((tile % 4) * tile_cols).astype(jnp.int32)
        patch_block = lax.dynamic_slice(padded, (jnp.int32(0), anchor_row, anchor_col), (channels, tile_rows + 2 * margin, tile_cols + 2 * margin)).astype(jnp.float32)
        row_weights = rounded(cubic_weights(row_fracs[tile]))
        col_weights = rounded(cubic_weights(col_fracs[tile]))
        row_first = first_rows[tile].astype(jnp.int32)
        col_first = first_cols[tile].astype(jnp.int32)
        row_segment = jnp.zeros((channels, out_rows, tile_cols + 2 * margin), jnp.float32)
        for tap_shift in range(4):
            row_segment = row_segment + patch_block[:, row_first + tap_shift, :] * row_weights[tap_shift][None, :, None]
        row_segment = rounded(row_segment)
        result = jnp.zeros((channels, out_rows, out_cols), jnp.float32)
        for tap_shift in range(4):
            result = result + row_segment[:, :, col_first + tap_shift] * col_weights[tap_shift][None, None, :]
        return result.astype(jnp.bfloat16)

    return lax.map(one_tile, jnp.arange(tiles_all, dtype=jnp.int32))


def reference(pan_source, ms_source, row_tap, row_frac, col_tap, col_frac, ms_row_tap, ms_row_frac, ms_col_tap, ms_col_frac):
    pan_source = jnp.roll(pan_source, 2, axis=0)
    ms_source = jnp.roll(ms_source, 2, axis=1)
    row_tap = jnp.roll(row_tap, 2, axis=0)
    row_frac = jnp.roll(row_frac, 2, axis=0)
    col_tap = jnp.roll(col_tap, 2, axis=0)
    col_frac = jnp.roll(col_frac, 2, axis=0)
    ms_row_tap = jnp.roll(ms_row_tap, 2, axis=0)
    ms_row_frac = jnp.roll(ms_row_frac, 2, axis=0)
    ms_col_tap = jnp.roll(ms_col_tap, 2, axis=0)
    ms_col_frac = jnp.roll(ms_col_frac, 2, axis=0)
    tiles_all = pan_source.shape[0]
    tile_rows = pan_source.shape[1]
    tile_cols = pan_source.shape[2]
    grid_rows = tiles_all // 4
    map_rows = grid_rows * tile_rows
    map_cols = 4 * tile_cols
    pan_tiles = resample_all(pan_source[None], row_tap, row_frac, col_tap, col_frac, HALO, tile_rows, tile_cols)
    ms_tiles = resample_all(ms_source, ms_row_tap, ms_row_frac, ms_col_tap, ms_col_frac, MHALO, tile_rows, tile_cols)
    tiles = jnp.concatenate([pan_tiles, ms_tiles], axis=1)
    channels = tiles.shape[1]
    resampled = tiles.reshape(grid_rows, 4, channels, tile_rows, tile_cols).transpose(2, 0, 3, 1, 4).reshape(channels, map_rows, map_cols)
    window = 2 * RADIUS + 1

    def box(values):
        widened = jnp.pad(values, ((RADIUS, RADIUS), (RADIUS, RADIUS)))
        return window_sum(window_sum(widened, 0, window), 1, window)

    row_cover = coverage(jnp.int32(0), map_rows, map_rows, RADIUS)
    col_cover = coverage(jnp.int32(0), map_cols, map_cols, RADIUS)
    coverage_map = row_cover[:, None] * col_cover[None, :]
    guide_image = resampled[0].astype(jnp.float32)
    mean_guide = box(guide_image) / coverage_map
    mean_square = box(guide_image * guide_image) / coverage_map
    variance = mean_square - mean_guide * mean_guide

    def one_band(band_image):
        values = band_image.astype(jnp.float32)
        mean_band = box(values) / coverage_map
        mean_cross = box(guide_image * values) / coverage_map
        gain_map = (mean_cross - mean_guide * mean_band) / (variance + EPSILON)
        offset_map = mean_band - gain_map * mean_guide
        gain_map = rounded(gain_map)
        offset_map = rounded(offset_map)
        return (box(gain_map) / coverage_map * guide_image + box(offset_map) / coverage_map).astype(jnp.bfloat16)

    sharpened = lax.map(one_band, resampled[1:])
    bands = sharpened.shape[0]
    placed = sharpened.reshape(bands, grid_rows, tile_rows, 4, tile_cols).transpose(0, 1, 3, 2, 4).reshape(bands, tiles_all, tile_rows, tile_cols)
    return jnp.roll(placed, -2, axis=1)
```

```python
import functools

import jax
import jax.numpy as jnp
from jax import lax
from jax.experimental import pallas as pl
from jax.experimental.pallas import tpu as pltpu
from jax.sharding import PartitionSpec as P

HALO = 32
MHALO = 8
RADIUS = 8
EPSILON = 0.1
GRID_COLS = 4
EDGE = 2 * RADIUS
LANES = 128
MESH = pl.DeviceIdType.MESH

STEPS = ((1, 0), (-1, 0), (0, 1), (0, -1), (1, 1), (1, -1), (-1, 1), (-1, -1))


def cubic_weights(fraction):
    squared = fraction * fraction
    cubed = squared * fraction
    return (
        -0.5 * cubed + squared - 0.5 * fraction,
        1.5 * cubed - 2.5 * squared + 1.0,
        -1.5 * cubed + 2.0 * squared + 0.5 * fraction,
        0.5 * cubed - 0.5 * squared,
    )


def band(taps, fraction, length, shift):
    weights = cubic_weights(fraction)
    outputs = taps.shape[1]
    distance = lax.broadcasted_iota(jnp.int32, (length, outputs), 0) - (taps + shift)
    matrix = jnp.zeros((length, outputs), jnp.float32)
    for offset in range(4):
        matrix = jnp.where(distance == offset, weights[offset], matrix)
    return matrix.astype(jnp.bfloat16)


def dot(left, right):
    return jnp.dot(left, right, preferred_element_type=jnp.float32)


def dot_t(left, right):
    return lax.dot_general(
        left, right, (((0,), (0,)), ((), ())), preferred_element_type=jnp.float32
    )


def place(sec_count, tile_count):
    total = sec_count * tile_count
    me = lax.axis_index("sec") * tile_count + lax.axis_index("tile")
    return lax.rem(me + 2, total), total


def resample_kernel(
    sec_count,
    tile_count,
    pan,
    ms,
    row_tap,
    row_frac,
    col_tap,
    col_frac,
    ms_row_tap,
    ms_row_frac,
    ms_col_tap,
    ms_col_frac,
    wide,
    pan_patch,
    ms_side,
    ms_vert,
    ms_corner,
    pack_east,
    pack_west,
    got_west,
    got_east,
    local_sem,
    send_pan,
    recv_pan,
    send_ms,
    recv_ms,
    send_edge,
    recv_edge,
):
    rows, cols = pan.shape
    bands, ms_rows, ms_cols = ms.shape
    channels = bands + 1
    placed, total = place(sec_count, tile_count)
    column = lax.rem(placed, GRID_COLS)
    grid_row = placed // GRID_COLS
    north_ok = grid_row > 0
    south_ok = grid_row < total // GRID_COLS - 1
    west_ok = column > 0
    east_ok = column < GRID_COLS - 1

    def device(down, right):
        there = lax.rem(placed + down * GRID_COLS + right - 2 + 2 * total, total)
        return (there // tile_count, lax.rem(there, tile_count))

    barrier = pltpu.get_barrier_semaphore()
    for down, right in STEPS:
        pl.semaphore_signal(
            barrier, inc=1, device_id=device(down, right), device_id_type=MESH
        )
    own = pltpu.make_async_copy(
        pan, pan_patch.at[HALO : HALO + rows, LANES : LANES + cols], local_sem
    )
    own.start()
    pl.semaphore_wait(barrier, len(STEPS))

    def span(step, size, depth):
        if step > 0:
            return slice(size - depth, size), slice(0, depth)
        if step < 0:
            return slice(0, depth), slice(depth + size, 2 * depth + size)
        return slice(0, size), slice(depth, depth + size)

    copies = []
    for index, (down, right) in enumerate(STEPS):
        row_from, row_to = span(down, rows, HALO)
        col_from, col_to = span(right, cols, LANES)
        copies.append(
            pltpu.make_async_remote_copy(
                src_ref=pan.at[row_from, col_from],
                dst_ref=pan_patch.at[row_to, col_to],
                send_sem=send_pan.at[index],
                recv_sem=recv_pan.at[index],
                device_id=device(down, right),
                device_id_type=MESH,
            )
        )
        if down == 0:
            source, target = ms, ms_side.at[0 if right > 0 else 1]
        else:
            source = ms.at[:, slice(ms_rows - 16, ms_rows) if down > 0 else slice(0, 16), :]
            if right == 0:
                target = ms_vert.at[0 if down > 0 else 1]
            else:
                target = ms_corner.at[(0 if right > 0 else 1) + (0 if down > 0 else 2)]
        copies.append(
            pltpu.make_async_remote_copy(
                src_ref=source,
                dst_ref=target,
                send_sem=send_ms.at[index],
                recv_sem=recv_ms.at[index],
                device_id=device(down, right),
                device_id_type=MESH,
            )
        )
    for copy in copies:
        copy.start()

    row_matrix = band(row_tap[...], row_frac[...], 2 * HALO + rows, 0)
    col_matrix = band(col_tap[...], col_frac[...], 2 * LANES + cols, LANES - HALO)
    ms_row_matrix = band(ms_row_tap[...], ms_row_frac[...], 32 + ms_rows, 16 - MHALO)
    ms_own_matrix = band(ms_col_tap[...], ms_col_frac[...], ms_cols, -MHALO)
    ms_west_matrix = band(ms_col_tap[...], ms_col_frac[...], ms_cols, ms_cols - MHALO)
    ms_east_matrix = band(ms_col_tap[...], ms_col_frac[...], ms_cols, -MHALO - ms_cols)

    own.wait()
    for copy in copies:
        copy.wait()

    def clear(ok, ref):
        @pl.when(jnp.logical_not(ok))
        def _():
            ref[...] = jnp.zeros(ref.shape, ref.dtype)

    clear(north_ok, pan_patch.at[:HALO, :])
    clear(south_ok, pan_patch.at[HALO + rows :, :])
    clear(west_ok, pan_patch.at[:, :LANES])
    clear(east_ok, pan_patch.at[:, LANES + cols :])
    clear(north_ok, ms_vert.at[0])
    clear(south_ok, ms_vert.at[1])
    clear(west_ok, ms_side.at[0])
    clear(east_ok, ms_side.at[1])
    for index, ok in enumerate(
        (north_ok & west_ok, north_ok & east_ok, south_ok & west_ok, south_ok & east_ok)
    ):
        clear(ok, ms_corner.at[index])

    segment = dot_t(row_matrix, pan_patch[...]).astype(jnp.bfloat16)
    wide[0, EDGE : EDGE + rows, :cols] = dot(segment, col_matrix).astype(jnp.bfloat16)
    for b in range(bands):
        parts = []
        for north, middle, south, matrix in (
            (ms_vert[0, b], ms[b], ms_vert[1, b], ms_own_matrix),
            (ms_corner[0, b], ms_side[0, b], ms_corner[2, b], ms_west_matrix),
            (ms_corner[1, b], ms_side[1, b], ms_corner[3, b], ms_east_matrix),
        ):
            block = jnp.concatenate([north, middle, south], axis=0)
            segment = dot_t(ms_row_matrix, block).astype(jnp.bfloat16)
            parts.append(dot(segment, matrix))
        wide[b + 1, EDGE : EDGE + rows, :cols] = (parts[0] + parts[1] + parts[2]).astype(
            jnp.bfloat16
        )

    lane = lax.broadcasted_iota(jnp.int32, (LANES, 2 * LANES), 0)
    slot = lax.broadcasted_iota(jnp.int32, (LANES, 2 * LANES), 1)
    east_sum = jnp.zeros((rows, 2 * LANES), jnp.float32)
    west_sum = jnp.zeros((rows, 2 * LANES), jnp.float32)
    for c in range(channels):
        pick = slot - c * EDGE
        inside = (pick >= 0) & (pick < EDGE)
        last = jnp.where(inside & (lane - (LANES - EDGE) == pick), 1.0, 0.0).astype(jnp.bfloat16)
        first = jnp.where(inside & (lane == pick), 1.0, 0.0).astype(jnp.bfloat16)
        east_sum = east_sum + dot(wide[c, EDGE : EDGE + rows, cols - LANES : cols], last)
        west_sum = west_sum + dot(wide[c, EDGE : EDGE + rows, :LANES], first)
    pack_east[...] = east_sum.astype(jnp.bfloat16)
    pack_west[...] = west_sum.astype(jnp.bfloat16)

    copies = []
    for index, (down, right) in enumerate(STEPS):
        row_from, row_to = span(down, rows, EDGE)
        if right == 0:
            source = wide.at[:, slice(row_from.start + EDGE, row_from.stop + EDGE), :cols]
            target = wide.at[:, row_to, :cols]
        elif right > 0:
            source, target = pack_east.at[row_from, :], got_west.at[row_to, :]
        else:
            source, target = pack_west.at[row_from, :], got_east.at[row_to, :]
        copies.append(
            pltpu.make_async_remote_copy(
                src_ref=source,
                dst_ref=target,
                send_sem=send_edge.at[index],
                recv_sem=recv_edge.at[index],
                device_id=device(down, right),
                device_id_type=MESH,
            )
        )
    for copy in copies:
        copy.start()
    for copy in copies:
        copy.wait()

    clear(north_ok, wide.at[:, :EDGE, :cols])
    clear(south_ok, wide.at[:, EDGE + rows :, :cols])
    for got, ok in ((got_west, west_ok), (got_east, east_ok)):
        clear(ok, got)
        clear(north_ok, got.at[:EDGE, :])
        clear(south_ok, got.at[EDGE + rows :, :])
    source = lax.broadcasted_iota(jnp.int32, (2 * LANES, LANES), 0)
    lane = lax.broadcasted_iota(jnp.int32, (2 * LANES, LANES), 1)
    for c in range(channels):
        pick = source - c * EDGE
        inside = (pick >= 0) & (pick < EDGE)
        from_east = jnp.where(inside & (lane == pick), 1.0, 0.0).astype(jnp.bfloat16)
        from_west = jnp.where(inside & (lane - (LANES - EDGE) == pick), 1.0, 0.0).astype(
            jnp.bfloat16
        )
        wide[c, :, cols:] = (
            dot(got_east[...], from_east) + dot(got_west[...], from_west)
        ).astype(jnp.bfloat16)


def sum_down(values, kept):
    count = values.shape[0]
    total = values
    for shift in (1, 2, 4):
        total = total + pltpu.roll(total, count - shift, 0)
    return total[:kept] + total[8 : kept + 8] + values[16 : kept + 16]


def inverse_cover(first, shape, axis, extent, kept):
    line = lax.broadcasted_iota(jnp.int32, shape, axis)
    places = line + first
    highest = jnp.minimum(places + RADIUS, extent - 1)
    lowest = jnp.maximum(places - RADIUS, 0)
    inside = (places >= 0) & (places < extent) & (line < kept)
    cover = jnp.where(inside, highest - lowest + 1, 1).astype(jnp.float32)
    return jnp.where(inside, 1.0 / cover, 0.0)


def filter_kernel(
    sec_count,
    tile_count,
    guide,
    bandref,
    out,
    box_a,
    box_b,
    inverse,
    inverse_out,
    mean_guide,
    inverse_var,
    sums_a,
    sums_b,
    fit_a,
    fit_b,
):
    wide_rows, width = guide.shape[1:]
    rows, cols = out.shape[1:]
    fit_rows = rows + EDGE
    chunks = width // LANES

    def box_across(values, matrix):
        high = values.astype(jnp.bfloat16)
        low = (values - high.astype(jnp.float32)).astype(jnp.bfloat16)
        return dot(high, matrix) + dot(low, matrix)

    @pl.when(pl.program_id(0) == 0)
    def _():
        placed, total = place(sec_count, tile_count)
        column = lax.rem(placed, GRID_COLS)
        grid_row = placed // GRID_COLS
        map_rows = total // GRID_COLS * rows
        map_cols = GRID_COLS * cols
        k = lax.broadcasted_iota(jnp.int32, (width, width), 0)
        j = lax.broadcasted_iota(jnp.int32, (width, width), 1)
        back = j - k
        back = jnp.where(back < 0, back + width, back)
        box_a[...] = jnp.where(back <= EDGE, 1.0, 0.0).astype(jnp.bfloat16)
        k = lax.broadcasted_iota(jnp.int32, (width, cols), 0)
        j = lax.broadcasted_iota(jnp.int32, (width, cols), 1)
        box_b[...] = jnp.where((k >= j) & (k - j <= EDGE), 1.0, 0.0).astype(jnp.bfloat16)
        row0 = grid_row * rows
        col0 = column * cols
        inverse[...] = inverse_cover(
            row0 - RADIUS, (fit_rows, width), 0, map_rows, fit_rows
        ) * inverse_cover(col0 - RADIUS, (fit_rows, width), 1, map_cols, cols + EDGE)
        inverse_out[...] = inverse_cover(row0, (rows, cols), 0, map_rows, rows) * inverse_cover(
            col0, (rows, cols), 1, map_cols, cols
        )
        own = guide[0].astype(jnp.float32)
        sums_a[...] = dot(guide[0], box_a[...])
        sums_b[...] = box_across(own * own, box_a[...])
        for t in range(chunks):
            lanes = slice(t * LANES, (t + 1) * LANES)
            scale = inverse[:, lanes]
            mean = sum_down(sums_a[:, lanes], fit_rows) * scale
            square = sum_down(sums_b[:, lanes], fit_rows) * scale
            mean_guide[:, lanes] = mean
            inverse_var[:, lanes] = 1.0 / (square - mean * mean + EPSILON)

    sums_a[...] = dot(bandref[0], box_a[...])
    sums_b[...] = box_across(
        guide[0].astype(jnp.float32) * bandref[0].astype(jnp.float32), box_a[...]
    )
    for t in range(chunks):
        lanes = slice(t * LANES, (t + 1) * LANES)
        scale = inverse[:, lanes]
        mean = mean_guide[:, lanes]
        mean_band = sum_down(sums_a[:, lanes], fit_rows) * scale
        cross = sum_down(sums_b[:, lanes], fit_rows) * scale
        gain = (cross - mean * mean_band) * inverse_var[:, lanes]
        fit_a[:, lanes] = gain.astype(jnp.bfloat16)
        fit_b[:, lanes] = (mean_band - gain * mean).astype(jnp.bfloat16)
    sums_a[:fit_rows, :cols] = dot(fit_a[...], box_b[...])
    sums_b[:fit_rows, :cols] = dot(fit_b[...], box_b[...])
    for t in range(cols // LANES):
        lanes = slice(t * LANES, (t + 1) * LANES)
        own = guide[0, EDGE : EDGE + rows, lanes].astype(jnp.float32)
        gain = sum_down(sums_a[:fit_rows, lanes], rows)
        offset = sum_down(sums_b[:fit_rows, lanes], rows)
        out[0, :, lanes] = ((gain * own + offset) * inverse_out[:, lanes]).astype(jnp.bfloat16)


def local(sec_count, tile_count, pan_source, ms_source, *tables):
    rows, cols = pan_source.shape[1:]
    bands, _, ms_rows, ms_cols = ms_source.shape
    channels = bands + 1
    wide_rows = rows + 2 * EDGE
    width = cols + LANES
    bf16, f32 = jnp.bfloat16, jnp.float32
    vmem = pl.BlockSpec(memory_space=pltpu.VMEM)
    dma = pltpu.SemaphoreType.DMA
    wide = pl.pallas_call(
        functools.partial(resample_kernel, sec_count, tile_count),
        out_shape=jax.ShapeDtypeStruct((channels, wide_rows, width), bf16),
        in_specs=[vmem] * (2 + len(tables)),
        out_specs=vmem,
        scratch_shapes=[
            pltpu.VMEM((rows + 2 * HALO, cols + 2 * LANES), bf16),
            pltpu.VMEM((2, bands, ms_rows, ms_cols), bf16),
            pltpu.VMEM((2, bands, 16, ms_cols), bf16),
            pltpu.VMEM((4, bands, 16, ms_cols), bf16),
            pltpu.VMEM((rows, 2 * LANES), bf16),
            pltpu.VMEM((rows, 2 * LANES), bf16),
            pltpu.VMEM((wide_rows, 2 * LANES), bf16),
            pltpu.VMEM((wide_rows, 2 * LANES), bf16),
            dma,
        ]
        + [dma((len(STEPS),))] * 6,
        compiler_params=pltpu.CompilerParams(
            collective_id=0, has_side_effects=True, vmem_limit_bytes=48 * 2**20
        ),
    )(pan_source.reshape(rows, cols), ms_source.reshape(bands, ms_rows, ms_cols), *tables)
    fit_rows = rows + EDGE
    sharpened = pl.pallas_call(
        functools.partial(filter_kernel, sec_count, tile_count),
        grid=(bands,),
        out_shape=jax.ShapeDtypeStruct((bands, rows, cols), bf16),
        in_specs=[
            pl.BlockSpec((1, wide_rows, width), lambda b: (0, 0, 0)),
            pl.BlockSpec((1, wide_rows, width), lambda b: (b + 1, 0, 0)),
        ],
        out_specs=pl.BlockSpec((1, rows, cols), lambda b: (b, 0, 0)),
        scratch_shapes=[
            pltpu.VMEM((width, width), bf16),
            pltpu.VMEM((width, cols), bf16),
            pltpu.VMEM((fit_rows, width), f32),
            pltpu.VMEM((rows, cols), f32),
            pltpu.VMEM((fit_rows, width), f32),
            pltpu.VMEM((fit_rows, width), f32),
            pltpu.VMEM((wide_rows, width), f32),
            pltpu.VMEM((wide_rows, width), f32),
            pltpu.VMEM((fit_rows, width), bf16),
            pltpu.VMEM((fit_rows, width), bf16),
        ],
        compiler_params=pltpu.CompilerParams(vmem_limit_bytes=48 * 2**20),
    )(wide, wide)
    return sharpened[:, None]


def solution(mesh):
    tiles = ("sec", "tile")
    table = P(tiles, None)
    return jax.shard_map(
        functools.partial(local, mesh.shape["sec"], mesh.shape["tile"]),
        mesh=mesh,
        in_specs=(P(tiles, None, None), P(None, tiles, None, None)) + (table,) * 8,
        out_specs=P(None, tiles, None, None),
        check_vma=False,
    )
```

```python
import functools

import jax
import jax.numpy as jnp
from jax import lax
from jax.experimental import pallas as pl
from jax.experimental.pallas import tpu as pltpu
from jax.sharding import PartitionSpec as P

HALO = 32
MHALO = 8
RADIUS = 8
EPSILON = 0.1
GRID_COLS = 4
EDGE = 2 * RADIUS
LANES = 128
MESH = pl.DeviceIdType.MESH

STEPS = ((1, 0), (-1, 0), (0, 1), (0, -1), (1, 1), (1, -1), (-1, 1), (-1, -1))


def cubic_weights(fraction):
    squared = fraction * fraction
    cubed = squared * fraction
    return (
        -0.5 * cubed + squared - 0.5 * fraction,
        1.5 * cubed - 2.5 * squared + 1.0,
        -1.5 * cubed + 2.0 * squared + 0.5 * fraction,
        0.5 * cubed - 0.5 * squared,
    )


def band(taps, fraction, length, shift):
    line = lax.broadcasted_iota(jnp.int32, (length, taps.shape[1]), 0)
    return band_at(line - shift, taps, fraction)


def band_at(position, taps, fraction):
    weights = cubic_weights(fraction)
    distance = position - taps
    matrix = jnp.zeros(position.shape, jnp.float32)
    for offset in range(4):
        matrix = jnp.where(distance == offset, weights[offset], matrix)
    return matrix.astype(jnp.bfloat16)


def picker(shape, shift, low, high):
    source = lax.broadcasted_iota(jnp.int32, shape, 0)
    target = lax.broadcasted_iota(jnp.int32, shape, 1)
    chosen = (target - source == shift) & (source >= low) & (source < high)
    return jnp.where(chosen, 1.0, 0.0).astype(jnp.bfloat16)


def dot(left, right):
    return jnp.dot(left, right, preferred_element_type=jnp.float32)


def dot_t(left, right):
    return lax.dot_general(
        left, right, (((0,), (0,)), ((), ())), preferred_element_type=jnp.float32
    )


def place(sec_count, tile_count):
    total = sec_count * tile_count
    me = lax.axis_index("sec") * tile_count + lax.axis_index("tile")
    return lax.rem(me + 2, total), total


def resample_kernel(
    sec_count,
    tile_count,
    pan,
    ms,
    row_tap,
    row_frac,
    col_tap,
    col_frac,
    ms_row_tap,
    ms_row_frac,
    ms_col_tap,
    ms_col_frac,
    wide,
    ms_own,
    row_tap_here,
    row_frac_here,
    col_tap_here,
    col_frac_here,
    ms_row_tap_here,
    ms_row_frac_here,
    ms_col_tap_here,
    ms_col_frac_here,
    pan_patch,
    ms_vert,
    pan_pack,
    pan_got,
    ms_pack,
    ms_got,
    pack_east,
    pack_west,
    got_west,
    got_east,
    local_sem,
    table_sem,
    send_pan,
    recv_pan,
    send_ms,
    recv_ms,
    send_edge,
    recv_edge,
):
    rows, cols = pan.shape
    bands, ms_rows, ms_cols = ms.shape
    channels = bands + 1
    placed, total = place(sec_count, tile_count)
    column = lax.rem(placed, GRID_COLS)
    grid_row = placed // GRID_COLS
    north_ok = grid_row > 0
    south_ok = grid_row < total // GRID_COLS - 1
    west_ok = column > 0
    east_ok = column < GRID_COLS - 1

    def device(down, right):
        there = lax.rem(placed + down * GRID_COLS + right - 2 + 2 * total, total)
        return (there // tile_count, lax.rem(there, tile_count))

    def reaches(down, right):
        ok = True
        if down:
            ok = south_ok if down > 0 else north_ok
        if right:
            side = east_ok if right > 0 else west_ok
            ok = side if ok is True else ok & side
        return ok

    def start_all(steps, copies):
        for (down, right), copy in zip(steps, copies):
            pl.when(reaches(down, right))(copy.start)

    def wait_all(steps, copies):
        for (down, right), copy in zip(steps, copies):
            pl.when(reaches(-down, -right))(copy.wait_recv)
        for (down, right), copy in zip(steps, copies):
            pl.when(reaches(down, right))(copy.wait_send)

    barrier = pltpu.get_barrier_semaphore()
    for down, right in STEPS:

        @pl.when(reaches(down, right))
        def _(down=down, right=right):
            pl.semaphore_signal(
                barrier, inc=1, device_id=device(down, right), device_id_type=MESH
            )

    own = pltpu.make_async_copy(
        pan, pan_patch.at[HALO : HALO + rows, LANES : LANES + cols], local_sem
    )
    fetched = [
        pltpu.make_async_copy(source, target, table_sem.at[index])
        for index, (source, target) in enumerate(
            (
                (row_tap, row_tap_here),
                (row_frac, row_frac_here),
                (col_tap, col_tap_here),
                (col_frac, col_frac_here),
                (ms_row_tap, ms_row_tap_here),
                (ms_row_frac, ms_row_frac_here),
                (ms_col_tap, ms_col_tap_here),
                (ms_col_frac, ms_col_frac_here),
                (ms, ms_own),
            )
        )
    ]
    for copy in fetched:
        copy.start()
    own.start()
    for copy in fetched:
        copy.wait()
    own.wait()
    group = rows // (LANES // HALO)
    ms_slot = LANES // 2
    for side in range(2):
        total_pan = jnp.zeros((group, LANES), jnp.float32)
        first_lane = 0 if side else LANES - HALO
        block = slice(LANES, 2 * LANES) if side else slice(cols, cols + LANES)
        for g in range(LANES // HALO):
            move = picker(
                (LANES, LANES), g * HALO - first_lane, first_lane, first_lane + HALO
            )
            lines = slice(HALO + g * group, HALO + (g + 1) * group)
            total_pan = total_pan + dot(pan_patch[lines, block], move)
        pan_pack[side] = total_pan.astype(jnp.bfloat16)
        total_ms = jnp.zeros((ms_rows, LANES), jnp.float32)
        first_lane = 0 if side else ms_cols - MHALO
        for b in range(bands):
            move = picker(
                (ms_cols, LANES),
                side * ms_slot + b * MHALO - first_lane,
                first_lane,
                first_lane + MHALO,
            )
            total_ms = total_ms + dot(ms_own[b], move)
        ms_pack[side] = total_ms.astype(jnp.bfloat16)

    tall = 1 + north_ok.astype(jnp.int32) + south_ok.astype(jnp.int32)
    broad = 1 + west_ok.astype(jnp.int32) + east_ok.astype(jnp.int32)
    pl.semaphore_wait(barrier, tall * broad - 1)

    def span(step, size, depth):
        if step > 0:
            return slice(size - depth, size), slice(0, depth)
        if step < 0:
            return slice(0, depth), slice(depth + size, 2 * depth + size)
        return slice(0, size), slice(depth, depth + size)

    steps, copies = [], []
    for index, (down, right) in enumerate(STEPS):
        row_from, row_to = span(down, rows, HALO)
        col_from, col_to = span(right, cols, LANES)
        side = 0 if right > 0 else 1
        if down:
            source, target = pan.at[row_from, col_from], pan_patch.at[row_to, col_to]
        else:
            source, target = pan_pack.at[side], pan_got.at[side]
        steps.append((down, right))
        copies.append(
            pltpu.make_async_remote_copy(
                src_ref=source,
                dst_ref=target,
                send_sem=send_pan.at[index],
                recv_sem=recv_pan.at[index],
                device_id=device(down, right),
                device_id_type=MESH,
            )
        )
        row_from, row_to = span(down, ms_rows, 16)
        if right:
            source, target = ms_pack.at[side, row_from, :], ms_got.at[side, row_to, :]
        else:
            source, target = ms_own.at[:, row_from, :], ms_vert.at[0 if down > 0 else 1]
        steps.append((down, right))
        copies.append(
            pltpu.make_async_remote_copy(
                src_ref=source,
                dst_ref=target,
                send_sem=send_ms.at[index],
                recv_sem=recv_ms.at[index],
                device_id=device(down, right),
                device_id_type=MESH,
            )
        )
    start_all(steps, copies)
    row_matrix = band(row_tap_here[...], row_frac_here[...], 2 * HALO + rows, 0)
    col_matrix = band(col_tap_here[...], col_frac_here[...], 2 * LANES + cols, LANES - HALO)
    ms_row_matrix = band(ms_row_tap_here[...], ms_row_frac_here[...], 32 + ms_rows, 16 - MHALO)
    ms_col_taps = ms_col_tap_here[...]
    ms_col_fracs = ms_col_frac_here[...]
    ms_own_matrix = band(ms_col_taps, ms_col_fracs, ms_cols, -MHALO)
    lane = lax.broadcasted_iota(jnp.int32, (LANES, cols), 0)
    ms_halo_matrix = band_at(
        jnp.where(lane < ms_slot, 0, ms_cols + MHALO) + lax.rem(lane, MHALO),
        ms_col_taps,
        ms_col_fracs,
    )

    wait_all(steps, copies)

    def clear(ok, ref):
        @pl.when(jnp.logical_not(ok))
        def _():
            ref[...] = jnp.zeros(ref.shape, ref.dtype)

    clear(west_ok, pan_got.at[0])
    clear(east_ok, pan_got.at[1])
    for side in range(2):
        first_lane = 0 if side else LANES - HALO
        block = slice(LANES + cols, 2 * LANES + cols) if side else slice(0, LANES)
        for g in range(LANES // HALO):
            move = picker((LANES, LANES), first_lane - g * HALO, g * HALO, (g + 1) * HALO)
            lines = slice(HALO + g * group, HALO + (g + 1) * group)
            pan_patch[lines, block] = dot(pan_got[side], move).astype(jnp.bfloat16)

    clear(north_ok, pan_patch.at[:HALO, :])
    clear(south_ok, pan_patch.at[HALO + rows :, :])
    clear(west_ok, pan_patch.at[:, :LANES])
    clear(east_ok, pan_patch.at[:, LANES + cols :])
    clear(north_ok, ms_vert.at[0])
    clear(south_ok, ms_vert.at[1])
    for side, ok in ((0, west_ok), (1, east_ok)):
        clear(ok, ms_got.at[side])
        clear(north_ok, ms_got.at[side, :16, :])
        clear(south_ok, ms_got.at[side, 16 + ms_rows :, :])

    segment = dot_t(row_matrix, pan_patch[...]).astype(jnp.bfloat16)
    wide[0, EDGE : EDGE + rows, :cols] = dot(segment, col_matrix).astype(jnp.bfloat16)
    lane = lax.broadcasted_iota(jnp.int32, (rows, LANES), 1)
    halo_segment = dot_t(ms_row_matrix, ms_got[0]) + dot_t(ms_row_matrix, ms_got[1])
    halo_band = lax.rem(lane, ms_slot) // MHALO
    for b in range(bands):
        block = jnp.concatenate([ms_vert[0, b], ms_own[b], ms_vert[1, b]], axis=0)
        segment = dot_t(ms_row_matrix, block).astype(jnp.bfloat16)
        beside = jnp.where(halo_band == b, halo_segment, 0.0).astype(jnp.bfloat16)
        wide[b + 1, EDGE : EDGE + rows, :cols] = (
            dot(segment, ms_own_matrix) + dot(beside, ms_halo_matrix)
        ).astype(jnp.bfloat16)

    lane = lax.broadcasted_iota(jnp.int32, (LANES, 2 * LANES), 0)
    slot = lax.broadcasted_iota(jnp.int32, (LANES, 2 * LANES), 1)
    east_sum = jnp.zeros((rows, 2 * LANES), jnp.float32)
    west_sum = jnp.zeros((rows, 2 * LANES), jnp.float32)
    for c in range(channels):
        pick = slot - c * EDGE
        inside = (pick >= 0) & (pick < EDGE)
        last = jnp.where(inside & (lane - (LANES - EDGE) == pick), 1.0, 0.0).astype(jnp.bfloat16)
        first = jnp.where(inside & (lane == pick), 1.0, 0.0).astype(jnp.bfloat16)
        east_sum = east_sum + dot(wide[c, EDGE : EDGE + rows, cols - LANES : cols], last)
        west_sum = west_sum + dot(wide[c, EDGE : EDGE + rows, :LANES], first)
    pack_east[...] = east_sum.astype(jnp.bfloat16)
    pack_west[...] = west_sum.astype(jnp.bfloat16)

    copies = []
    for index, (down, right) in enumerate(STEPS):
        row_from, row_to = span(down, rows, EDGE)
        if right == 0:
            source = wide.at[:, slice(row_from.start + EDGE, row_from.stop + EDGE), :cols]
            target = wide.at[:, row_to, :cols]
        elif right > 0:
            source, target = pack_east.at[row_from, :], got_west.at[row_to, :]
        else:
            source, target = pack_west.at[row_from, :], got_east.at[row_to, :]
        copies.append(
            pltpu.make_async_remote_copy(
                src_ref=source,
                dst_ref=target,
                send_sem=send_edge.at[index],
                recv_sem=recv_edge.at[index],
                device_id=device(down, right),
                device_id_type=MESH,
            )
        )
    start_all(STEPS, copies)
    wait_all(STEPS, copies)

    clear(north_ok, wide.at[:, :EDGE, :cols])
    clear(south_ok, wide.at[:, EDGE + rows :, :cols])
    for got, ok in ((got_west, west_ok), (got_east, east_ok)):
        clear(ok, got)
        clear(north_ok, got.at[:EDGE, :])
        clear(south_ok, got.at[EDGE + rows :, :])
    source = lax.broadcasted_iota(jnp.int32, (2 * LANES, LANES), 0)
    lane = lax.broadcasted_iota(jnp.int32, (2 * LANES, LANES), 1)
    for c in range(channels):
        pick = source - c * EDGE
        inside = (pick >= 0) & (pick < EDGE)
        from_east = jnp.where(inside & (lane == pick), 1.0, 0.0).astype(jnp.bfloat16)
        from_west = jnp.where(inside & (lane - (LANES - EDGE) == pick), 1.0, 0.0).astype(
            jnp.bfloat16
        )
        wide[c, :, cols:] = (
            dot(got_east[...], from_east) + dot(got_west[...], from_west)
        ).astype(jnp.bfloat16)


def sum_down(values, kept):
    count = values.shape[0]
    total = values
    for shift in (1, 2, 4):
        total = total + pltpu.roll(total, count - shift, 0)
    return total[:kept] + total[8 : kept + 8] + values[16 : kept + 16]


def inverse_cover(first, shape, axis, extent, kept):
    line = lax.broadcasted_iota(jnp.int32, shape, axis)
    places = line + first
    highest = jnp.minimum(places + RADIUS, extent - 1)
    lowest = jnp.maximum(places - RADIUS, 0)
    inside = (places >= 0) & (places < extent) & (line < kept)
    cover = jnp.where(inside, highest - lowest + 1, 1).astype(jnp.float32)
    return jnp.where(inside, 1.0 / cover, 0.0)


def filter_kernel(
    sec_count,
    tile_count,
    guide,
    bandref,
    out,
    box_a,
    box_b,
    inverse,
    inverse_out,
    mean_guide,
    inverse_var,
    sums_a,
    sums_b,
    fit_a,
    fit_b,
):
    wide_rows, width = guide.shape[1:]
    rows, cols = out.shape[1:]
    fit_rows = rows + EDGE
    chunks = width // LANES

    def box_across(values, matrix):
        high = values.astype(jnp.bfloat16)
        low = (values - high.astype(jnp.float32)).astype(jnp.bfloat16)
        return dot(high, matrix) + dot(low, matrix)

    @pl.when(pl.program_id(0) == 0)
    def _():
        placed, total = place(sec_count, tile_count)
        column = lax.rem(placed, GRID_COLS)
        grid_row = placed // GRID_COLS
        map_rows = total // GRID_COLS * rows
        map_cols = GRID_COLS * cols
        k = lax.broadcasted_iota(jnp.int32, (width, width), 0)
        j = lax.broadcasted_iota(jnp.int32, (width, width), 1)
        back = j - k
        back = jnp.where(back < 0, back + width, back)
        box_a[...] = jnp.where(back <= EDGE, 1.0, 0.0).astype(jnp.bfloat16)
        k = lax.broadcasted_iota(jnp.int32, (width, cols), 0)
        j = lax.broadcasted_iota(jnp.int32, (width, cols), 1)
        box_b[...] = jnp.where((k >= j) & (k - j <= EDGE), 1.0, 0.0).astype(jnp.bfloat16)
        row0 = grid_row * rows
        col0 = column * cols
        inverse[...] = inverse_cover(
            row0 - RADIUS, (fit_rows, width), 0, map_rows, fit_rows
        ) * inverse_cover(col0 - RADIUS, (fit_rows, width), 1, map_cols, cols + EDGE)
        inverse_out[...] = inverse_cover(row0, (rows, cols), 0, map_rows, rows) * inverse_cover(
            col0, (rows, cols), 1, map_cols, cols
        )
        own = guide[0].astype(jnp.float32)
        sums_a[...] = dot(guide[0], box_a[...])
        sums_b[...] = box_across(own * own, box_a[...])
        for t in range(chunks):
            lanes = slice(t * LANES, (t + 1) * LANES)
            scale = inverse[:, lanes]
            mean = sum_down(sums_a[:, lanes], fit_rows) * scale
            square = sum_down(sums_b[:, lanes], fit_rows) * scale
            mean_guide[:, lanes] = mean
            inverse_var[:, lanes] = 1.0 / (square - mean * mean + EPSILON)

    sums_a[...] = dot(bandref[0], box_a[...])
    sums_b[...] = box_across(
        guide[0].astype(jnp.float32) * bandref[0].astype(jnp.float32), box_a[...]
    )
    for t in range(chunks):
        lanes = slice(t * LANES, (t + 1) * LANES)
        scale = inverse[:, lanes]
        mean = mean_guide[:, lanes]
        mean_band = sum_down(sums_a[:, lanes], fit_rows) * scale
        cross = sum_down(sums_b[:, lanes], fit_rows) * scale
        gain = (cross - mean * mean_band) * inverse_var[:, lanes]
        fit_a[:, lanes] = gain.astype(jnp.bfloat16)
        fit_b[:, lanes] = (mean_band - gain * mean).astype(jnp.bfloat16)
    sums_a[:fit_rows, :cols] = dot(fit_a[...], box_b[...])
    sums_b[:fit_rows, :cols] = dot(fit_b[...], box_b[...])
    for t in range(cols // LANES):
        lanes = slice(t * LANES, (t + 1) * LANES)
        own = guide[0, EDGE : EDGE + rows, lanes].astype(jnp.float32)
        gain = sum_down(sums_a[:fit_rows, lanes], rows)
        offset = sum_down(sums_b[:fit_rows, lanes], rows)
        out[0, :, lanes] = ((gain * own + offset) * inverse_out[:, lanes]).astype(jnp.bfloat16)


def local(sec_count, tile_count, pan_source, ms_source, *tables):
    rows, cols = pan_source.shape[1:]
    bands, _, ms_rows, ms_cols = ms_source.shape
    channels = bands + 1
    wide_rows = rows + 2 * EDGE
    width = cols + LANES
    bf16, f32 = jnp.bfloat16, jnp.float32
    vmem = pl.BlockSpec(memory_space=pltpu.VMEM)
    dma = pltpu.SemaphoreType.DMA
    wide = pl.pallas_call(
        functools.partial(resample_kernel, sec_count, tile_count),
        out_shape=jax.ShapeDtypeStruct((channels, wide_rows, width), bf16),
        in_specs=[pl.BlockSpec(memory_space=pltpu.HBM)] * (2 + len(tables)),
        out_specs=vmem,
        scratch_shapes=[pltpu.VMEM((bands, ms_rows, ms_cols), bf16)]
        + [pltpu.VMEM(table.shape, table.dtype) for table in tables]
        + [
            pltpu.VMEM((rows + 2 * HALO, cols + 2 * LANES), bf16),
            pltpu.VMEM((2, bands, 16, ms_cols), bf16),
            pltpu.VMEM((2, rows * HALO // LANES, LANES), bf16),
            pltpu.VMEM((2, rows * HALO // LANES, LANES), bf16),
            pltpu.VMEM((2, ms_rows, LANES), bf16),
            pltpu.VMEM((2, ms_rows + 32, LANES), bf16),
            pltpu.VMEM((rows, 2 * LANES), bf16),
            pltpu.VMEM((rows, 2 * LANES), bf16),
            pltpu.VMEM((wide_rows, 2 * LANES), bf16),
            pltpu.VMEM((wide_rows, 2 * LANES), bf16),
            dma,
            dma((len(tables) + 1,)),
        ]
        + [dma((len(STEPS),))] * 6,
        compiler_params=pltpu.CompilerParams(collective_id=0, has_side_effects=True),
    )(pan_source.reshape(rows, cols), ms_source.reshape(bands, ms_rows, ms_cols), *tables)
    fit_rows = rows + EDGE
    sharpened = pl.pallas_call(
        functools.partial(filter_kernel, sec_count, tile_count),
        grid=(bands,),
        out_shape=jax.ShapeDtypeStruct((bands, rows, cols), bf16),
        in_specs=[
            pl.BlockSpec((1, wide_rows, width), lambda b: (0, 0, 0)),
            pl.BlockSpec((1, wide_rows, width), lambda b: (b + 1, 0, 0)),
        ],
        out_specs=pl.BlockSpec((1, rows, cols), lambda b: (b, 0, 0)),
        scratch_shapes=[
            pltpu.VMEM((width, width), bf16),
            pltpu.VMEM((width, cols), bf16),
            pltpu.VMEM((fit_rows, width), f32),
            pltpu.VMEM((rows, cols), f32),
            pltpu.VMEM((fit_rows, width), f32),
            pltpu.VMEM((fit_rows, width), f32),
            pltpu.VMEM((wide_rows, width), f32),
            pltpu.VMEM((wide_rows, width), f32),
            pltpu.VMEM((fit_rows, width), bf16),
            pltpu.VMEM((fit_rows, width), bf16),
        ],
    )(wide, wide)
    return sharpened[:, None]


def solution(mesh):
    tiles = ("sec", "tile")
    table = P(tiles, None)
    return jax.shard_map(
        functools.partial(local, mesh.shape["sec"], mesh.shape["tile"]),
        mesh=mesh,
        in_specs=(P(tiles, None, None), P(None, tiles, None, None)) + (table,) * 8,
        out_specs=P(None, tiles, None, None),
        check_vma=False,
    )
```

```python
import functools

import jax
import jax.numpy as jnp
from jax import lax
from jax.experimental import pallas as pl
from jax.experimental.pallas import tpu as pltpu
from jax.sharding import PartitionSpec as P

HALO = 32
MHALO = 8
RADIUS = 8
EPSILON = 0.1
GRID_COLS = 4
EDGE = 2 * RADIUS
LANES = 128
MESH = pl.DeviceIdType.MESH

STEPS = ((1, 0), (-1, 0), (0, 1), (0, -1), (1, 1), (1, -1), (-1, 1), (-1, -1))


def cubic_weights(fraction):
    squared = fraction * fraction
    cubed = squared * fraction
    return (
        -0.5 * cubed + squared - 0.5 * fraction,
        1.5 * cubed - 2.5 * squared + 1.0,
        -1.5 * cubed + 2.0 * squared + 0.5 * fraction,
        0.5 * cubed - 0.5 * squared,
    )


def band(taps, fraction, length, shift):
    line = lax.broadcasted_iota(jnp.int32, (length, taps.shape[1]), 0)
    return band_at(line - shift, taps, fraction)


def band_at(position, taps, fraction):
    weights = cubic_weights(fraction)
    distance = position - taps
    matrix = jnp.zeros(position.shape, jnp.float32)
    for offset in range(4):
        matrix = jnp.where(distance == offset, weights[offset], matrix)
    return matrix.astype(jnp.bfloat16)


def picker(shape, shift, low, high):
    source = lax.broadcasted_iota(jnp.int32, shape, 0)
    target = lax.broadcasted_iota(jnp.int32, shape, 1)
    chosen = (target - source == shift) & (source >= low) & (source < high)
    return jnp.where(chosen, 1.0, 0.0).astype(jnp.bfloat16)


def dot(left, right):
    return jnp.dot(left, right, preferred_element_type=jnp.float32)


def dot_t(left, right):
    return lax.dot_general(
        left, right, (((0,), (0,)), ((), ())), preferred_element_type=jnp.float32
    )


def place(sec_count, tile_count):
    total = sec_count * tile_count
    me = lax.axis_index("sec") * tile_count + lax.axis_index("tile")
    return lax.rem(me + 2, total), total


def resample_kernel(
    sec_count,
    tile_count,
    pan,
    ms,
    row_tap,
    row_frac,
    col_tap,
    col_frac,
    ms_row_tap,
    ms_row_frac,
    ms_col_tap,
    ms_col_frac,
    wide,
    ms_own,
    row_tap_here,
    row_frac_here,
    col_tap_here,
    col_frac_here,
    ms_row_tap_here,
    ms_row_frac_here,
    ms_col_tap_here,
    ms_col_frac_here,
    pan_patch,
    ms_vert,
    ms_tall,
    pan_pack,
    pan_got,
    ms_pack,
    ms_got,
    pack_east,
    pack_west,
    got_west,
    got_east,
    local_sem,
    table_sem,
    send_pan,
    recv_pan,
    send_ms,
    recv_ms,
    send_edge,
    recv_edge,
    send_tall,
    recv_tall,
):
    rows, cols = pan.shape
    bands, ms_rows, ms_cols = ms.shape
    channels = bands + 1
    placed, total = place(sec_count, tile_count)
    column = lax.rem(placed, GRID_COLS)
    grid_row = placed // GRID_COLS
    north_ok = grid_row > 0
    south_ok = grid_row < total // GRID_COLS - 1
    west_ok = column > 0
    east_ok = column < GRID_COLS - 1

    def device(down, right):
        there = lax.rem(placed + down * GRID_COLS + right - 2 + 2 * total, total)
        return (there // tile_count, lax.rem(there, tile_count))

    def reaches(down, right):
        ok = True
        if down:
            ok = south_ok if down > 0 else north_ok
        if right:
            side = east_ok if right > 0 else west_ok
            ok = side if ok is True else ok & side
        return ok

    def start_all(steps, copies):
        for (down, right), copy in zip(steps, copies):
            pl.when(reaches(down, right))(copy.start)

    def wait_all(steps, copies):
        for (down, right), copy in zip(steps, copies):
            pl.when(reaches(-down, -right))(copy.wait_recv)
        for (down, right), copy in zip(steps, copies):
            pl.when(reaches(down, right))(copy.wait_send)

    barrier = pltpu.get_barrier_semaphore()
    for down, right in STEPS:

        @pl.when(reaches(down, right))
        def _(down=down, right=right):
            pl.semaphore_signal(
                barrier, inc=1, device_id=device(down, right), device_id_type=MESH
            )

    own = pltpu.make_async_copy(
        pan, pan_patch.at[HALO : HALO + rows, LANES : LANES + cols], local_sem
    )
    fetched = [
        pltpu.make_async_copy(source, target, table_sem.at[index])
        for index, (source, target) in enumerate(
            (
                (row_tap, row_tap_here),
                (row_frac, row_frac_here),
                (col_tap, col_tap_here),
                (col_frac, col_frac_here),
                (ms_row_tap, ms_row_tap_here),
                (ms_row_frac, ms_row_frac_here),
                (ms_col_tap, ms_col_tap_here),
                (ms_col_frac, ms_col_frac_here),
                (ms, ms_own),
            )
        )
    ]
    for copy in fetched:
        copy.start()
    own.start()
    for copy in fetched:
        copy.wait()
    own.wait()
    group = rows // (LANES // HALO)
    ms_slot = LANES // 2
    for side in range(2):
        total_pan = jnp.zeros((group, LANES), jnp.float32)
        first_lane = 0 if side else LANES - HALO
        block = slice(LANES, 2 * LANES) if side else slice(cols, cols + LANES)
        for g in range(LANES // HALO):
            move = picker(
                (LANES, LANES), g * HALO - first_lane, first_lane, first_lane + HALO
            )
            lines = slice(HALO + g * group, HALO + (g + 1) * group)
            total_pan = total_pan + dot(pan_patch[lines, block], move)
        pan_pack[side] = total_pan.astype(jnp.bfloat16)
        total_ms = jnp.zeros((ms_rows, LANES), jnp.float32)
        first_lane = 0 if side else ms_cols - MHALO
        for b in range(bands):
            move = picker(
                (ms_cols, LANES),
                side * ms_slot + b * MHALO - first_lane,
                first_lane,
                first_lane + MHALO,
            )
            total_ms = total_ms + dot(ms_own[b], move)
        ms_pack[side] = total_ms.astype(jnp.bfloat16)
        lines = slice(0, MHALO) if side else slice(ms_rows - MHALO, ms_rows)
        for pair in range(bands // 2):
            both = [ms_own[b].astype(jnp.float32)[lines] for b in (2 * pair, 2 * pair + 1)]
            ms_tall[side, pair] = jnp.concatenate(both, axis=0).astype(jnp.bfloat16)

    tall = 1 + north_ok.astype(jnp.int32) + south_ok.astype(jnp.int32)
    broad = 1 + west_ok.astype(jnp.int32) + east_ok.astype(jnp.int32)
    pl.semaphore_wait(barrier, tall * broad - 1)

    def span(step, size, depth):
        if step > 0:
            return slice(size - depth, size), slice(0, depth)
        if step < 0:
            return slice(0, depth), slice(depth + size, 2 * depth + size)
        return slice(0, size), slice(depth, depth + size)

    steps, copies = [], []
    for index, (down, right) in enumerate(STEPS):
        row_from, row_to = span(down, rows, HALO)
        col_from, col_to = span(right, cols, LANES)
        side = 0 if right > 0 else 1
        if down:
            source, target = pan.at[row_from, col_from], pan_patch.at[row_to, col_to]
        else:
            source, target = pan_pack.at[side], pan_got.at[side]
        steps.append((down, right))
        copies.append(
            pltpu.make_async_remote_copy(
                src_ref=source,
                dst_ref=target,
                send_sem=send_pan.at[index],
                recv_sem=recv_pan.at[index],
                device_id=device(down, right),
                device_id_type=MESH,
            )
        )
        row_from, row_to = span(down, ms_rows, 16)
        if right:
            source, target = ms_pack.at[side, row_from, :], ms_got.at[side, row_to, :]
        else:
            source, target = ms_tall.at[0 if down > 0 else 1], ms_vert.at[0 if down > 0 else 1]
        steps.append((down, right))
        copies.append(
            pltpu.make_async_remote_copy(
                src_ref=source,
                dst_ref=target,
                send_sem=send_ms.at[index],
                recv_sem=recv_ms.at[index],
                device_id=device(down, right),
                device_id_type=MESH,
            )
        )
    start_all(steps, copies)
    row_matrix = band(row_tap_here[...], row_frac_here[...], 2 * HALO + rows, 0)
    col_matrix = band(col_tap_here[...], col_frac_here[...], 2 * LANES + cols, LANES - HALO)
    ms_row_taps = ms_row_tap_here[...]
    ms_row_fracs = ms_row_frac_here[...]
    ms_row_matrix = band(ms_row_taps, ms_row_fracs, 32 + ms_rows, 16 - MHALO)
    line = lax.broadcasted_iota(jnp.int32, (32 + ms_rows, rows), 0)
    below = 16 + ms_rows
    away = -LANES
    first_of_pair = jnp.where(
        line < MHALO, line, jnp.where((line < 16) | (line >= below + MHALO), away, line - MHALO)
    )
    second_of_pair = jnp.where(
        line < MHALO,
        away,
        jnp.where(
            line < below, line - MHALO, jnp.where(line < below + MHALO, away, line - 2 * MHALO)
        ),
    )
    ms_pair_matrices = tuple(
        band_at(position, ms_row_taps, ms_row_fracs)
        for position in (first_of_pair, second_of_pair)
    )
    ms_col_taps = ms_col_tap_here[...]
    ms_col_fracs = ms_col_frac_here[...]
    ms_own_matrix = band(ms_col_taps, ms_col_fracs, ms_cols, -MHALO)
    lane = lax.broadcasted_iota(jnp.int32, (LANES, cols), 0)
    ms_halo_matrix = band_at(
        jnp.where(lane < ms_slot, 0, ms_cols + MHALO) + lax.rem(lane, MHALO),
        ms_col_taps,
        ms_col_fracs,
    )

    wait_all(steps, copies)

    def clear(ok, ref):
        @pl.when(jnp.logical_not(ok))
        def _():
            ref[...] = jnp.zeros(ref.shape, ref.dtype)

    clear(west_ok, pan_got.at[0])
    clear(east_ok, pan_got.at[1])
    for side in range(2):
        first_lane = 0 if side else LANES - HALO
        block = slice(LANES + cols, 2 * LANES + cols) if side else slice(0, LANES)
        for g in range(LANES // HALO):
            move = picker((LANES, LANES), first_lane - g * HALO, g * HALO, (g + 1) * HALO)
            lines = slice(HALO + g * group, HALO + (g + 1) * group)
            pan_patch[lines, block] = dot(pan_got[side], move).astype(jnp.bfloat16)

    clear(north_ok, pan_patch.at[:HALO, :])
    clear(south_ok, pan_patch.at[HALO + rows :, :])
    clear(west_ok, pan_patch.at[:, :LANES])
    clear(east_ok, pan_patch.at[:, LANES + cols :])
    clear(north_ok, ms_vert.at[0])
    clear(south_ok, ms_vert.at[1])
    for side, ok in ((0, west_ok), (1, east_ok)):
        clear(ok, ms_got.at[side])
        clear(north_ok, ms_got.at[side, :16, :])
        clear(south_ok, ms_got.at[side, 16 + ms_rows :, :])

    tall_steps, tall_copies = [], []

    def send_rows(c):
        for index, down in enumerate((1, -1)):
            row_from, row_to = span(down, rows, EDGE)
            tall_steps.append((down, 0))
            tall_copies.append(
                pltpu.make_async_remote_copy(
                    src_ref=wide.at[c, slice(row_from.start + EDGE, row_from.stop + EDGE), :cols],
                    dst_ref=wide.at[c, row_to, :cols],
                    send_sem=send_tall.at[2 * c + index],
                    recv_sem=recv_tall.at[2 * c + index],
                    device_id=device(down, 0),
                    device_id_type=MESH,
                )
            )
        start_all(tall_steps[-2:], tall_copies[-2:])

    segment = dot_t(row_matrix, pan_patch[...]).astype(jnp.bfloat16)
    wide[0, EDGE : EDGE + rows, :cols] = dot(segment, col_matrix).astype(jnp.bfloat16)
    lane = lax.broadcasted_iota(jnp.int32, (rows, LANES), 1)
    halo_segment = dot_t(ms_row_matrix, ms_got[0]) + dot_t(ms_row_matrix, ms_got[1])
    halo_band = lax.rem(lane, ms_slot) // MHALO
    for b in range(bands):
        block = jnp.concatenate([ms_vert[0, b // 2], ms_own[b], ms_vert[1, b // 2]], axis=0)
        segment = dot_t(ms_pair_matrices[b % 2], block).astype(jnp.bfloat16)
        beside = jnp.where(halo_band == b, halo_segment, 0.0).astype(jnp.bfloat16)
        wide[b + 1, EDGE : EDGE + rows, :cols] = (
            dot(segment, ms_own_matrix) + dot(beside, ms_halo_matrix)
        ).astype(jnp.bfloat16)
        send_rows(b)

    lane = lax.broadcasted_iota(jnp.int32, (LANES, 2 * LANES), 0)
    slot = lax.broadcasted_iota(jnp.int32, (LANES, 2 * LANES), 1)
    east_sum = jnp.zeros((rows, 2 * LANES), jnp.float32)
    west_sum = jnp.zeros((rows, 2 * LANES), jnp.float32)
    for c in range(channels):
        pick = slot - c * EDGE
        inside = (pick >= 0) & (pick < EDGE)
        last = jnp.where(inside & (lane - (LANES - EDGE) == pick), 1.0, 0.0).astype(jnp.bfloat16)
        first = jnp.where(inside & (lane == pick), 1.0, 0.0).astype(jnp.bfloat16)
        east_sum = east_sum + dot(wide[c, EDGE : EDGE + rows, cols - LANES : cols], last)
        west_sum = west_sum + dot(wide[c, EDGE : EDGE + rows, :LANES], first)
    pack_east[...] = east_sum.astype(jnp.bfloat16)
    pack_west[...] = west_sum.astype(jnp.bfloat16)

    send_rows(bands)
    side_steps = tuple(step for step in STEPS if step[1])
    copies = []
    for index, (down, right) in enumerate(side_steps):
        row_from, row_to = span(down, rows, EDGE)
        if right > 0:
            source, target = pack_east.at[row_from, :], got_west.at[row_to, :]
        else:
            source, target = pack_west.at[row_from, :], got_east.at[row_to, :]
        copies.append(
            pltpu.make_async_remote_copy(
                src_ref=source,
                dst_ref=target,
                send_sem=send_edge.at[index],
                recv_sem=recv_edge.at[index],
                device_id=device(down, right),
                device_id_type=MESH,
            )
        )
    start_all(side_steps, copies)
    wait_all(tuple(tall_steps) + side_steps, tall_copies + copies)

    clear(north_ok, wide.at[:, :EDGE, :cols])
    clear(south_ok, wide.at[:, EDGE + rows :, :cols])
    for got, ok in ((got_west, west_ok), (got_east, east_ok)):
        clear(ok, got)
        clear(north_ok, got.at[:EDGE, :])
        clear(south_ok, got.at[EDGE + rows :, :])
    source = lax.broadcasted_iota(jnp.int32, (2 * LANES, LANES), 0)
    lane = lax.broadcasted_iota(jnp.int32, (2 * LANES, LANES), 1)
    for c in range(channels):
        pick = source - c * EDGE
        inside = (pick >= 0) & (pick < EDGE)
        from_east = jnp.where(inside & (lane == pick), 1.0, 0.0).astype(jnp.bfloat16)
        from_west = jnp.where(inside & (lane - (LANES - EDGE) == pick), 1.0, 0.0).astype(
            jnp.bfloat16
        )
        wide[c, :, cols:] = (
            dot(got_east[...], from_east) + dot(got_west[...], from_west)
        ).astype(jnp.bfloat16)


def sum_down(values, kept):
    count = values.shape[0]
    total = values
    for shift in (1, 2, 4):
        total = total + pltpu.roll(total, count - shift, 0)
    return total[:kept] + total[8 : kept + 8] + values[16 : kept + 16]


def inverse_cover(first, shape, axis, extent, kept):
    line = lax.broadcasted_iota(jnp.int32, shape, axis)
    places = line + first
    highest = jnp.minimum(places + RADIUS, extent - 1)
    lowest = jnp.maximum(places - RADIUS, 0)
    inside = (places >= 0) & (places < extent) & (line < kept)
    cover = jnp.where(inside, highest - lowest + 1, 1).astype(jnp.float32)
    return jnp.where(inside, 1.0 / cover, 0.0)


def filter_kernel(
    sec_count,
    tile_count,
    guide,
    bandref,
    out,
    box_a,
    box_b,
    inverse,
    inverse_out,
    mean_guide,
    inverse_var,
    sums_a,
    sums_b,
    fit_a,
    fit_b,
):
    wide_rows, width = guide.shape[1:]
    rows, cols = out.shape[1:]
    fit_rows = rows + EDGE
    chunks = width // LANES

    def box_across(values, matrix):
        high = values.astype(jnp.bfloat16)
        low = (values - high.astype(jnp.float32)).astype(jnp.bfloat16)
        return dot(high, matrix) + dot(low, matrix)

    @pl.when(pl.program_id(0) == 0)
    def _():
        placed, total = place(sec_count, tile_count)
        column = lax.rem(placed, GRID_COLS)
        grid_row = placed // GRID_COLS
        map_rows = total // GRID_COLS * rows
        map_cols = GRID_COLS * cols
        k = lax.broadcasted_iota(jnp.int32, (width, width), 0)
        j = lax.broadcasted_iota(jnp.int32, (width, width), 1)
        back = j - k
        back = jnp.where(back < 0, back + width, back)
        box_a[...] = jnp.where(back <= EDGE, 1.0, 0.0).astype(jnp.bfloat16)
        k = lax.broadcasted_iota(jnp.int32, (width, cols), 0)
        j = lax.broadcasted_iota(jnp.int32, (width, cols), 1)
        box_b[...] = jnp.where((k >= j) & (k - j <= EDGE), 1.0, 0.0).astype(jnp.bfloat16)
        row0 = grid_row * rows
        col0 = column * cols
        inverse[...] = inverse_cover(
            row0 - RADIUS, (fit_rows, width), 0, map_rows, fit_rows
        ) * inverse_cover(col0 - RADIUS, (fit_rows, width), 1, map_cols, cols + EDGE)
        inverse_out[...] = inverse_cover(row0, (rows, cols), 0, map_rows, rows) * inverse_cover(
            col0, (rows, cols), 1, map_cols, cols
        )
        own = guide[0].astype(jnp.float32)
        sums_a[...] = dot(guide[0], box_a[...])
        sums_b[...] = box_across(own * own, box_a[...])
        for t in range(chunks):
            lanes = slice(t * LANES, (t + 1) * LANES)
            scale = inverse[:, lanes]
            mean = sum_down(sums_a[:, lanes], fit_rows) * scale
            square = sum_down(sums_b[:, lanes], fit_rows) * scale
            mean_guide[:, lanes] = mean
            inverse_var[:, lanes] = 1.0 / (square - mean * mean + EPSILON)

    sums_a[...] = dot(bandref[0], box_a[...])
    sums_b[...] = box_across(
        guide[0].astype(jnp.float32) * bandref[0].astype(jnp.float32), box_a[...]
    )
    for t in range(chunks):
        lanes = slice(t * LANES, (t + 1) * LANES)
        scale = inverse[:, lanes]
        mean = mean_guide[:, lanes]
        mean_band = sum_down(sums_a[:, lanes], fit_rows) * scale
        cross = sum_down(sums_b[:, lanes], fit_rows) * scale
        gain = (cross - mean * mean_band) * inverse_var[:, lanes]
        fit_a[:, lanes] = gain.astype(jnp.bfloat16)
        fit_b[:, lanes] = (mean_band - gain * mean).astype(jnp.bfloat16)
    sums_a[:fit_rows, :cols] = dot(fit_a[...], box_b[...])
    sums_b[:fit_rows, :cols] = dot(fit_b[...], box_b[...])
    for t in range(cols // LANES):
        lanes = slice(t * LANES, (t + 1) * LANES)
        own = guide[0, EDGE : EDGE + rows, lanes].astype(jnp.float32)
        gain = sum_down(sums_a[:fit_rows, lanes], rows)
        offset = sum_down(sums_b[:fit_rows, lanes], rows)
        out[0, :, lanes] = ((gain * own + offset) * inverse_out[:, lanes]).astype(jnp.bfloat16)


def local(sec_count, tile_count, pan_source, ms_source, *tables):
    rows, cols = pan_source.shape[1:]
    bands, _, ms_rows, ms_cols = ms_source.shape
    channels = bands + 1
    wide_rows = rows + 2 * EDGE
    width = cols + LANES
    bf16, f32 = jnp.bfloat16, jnp.float32
    vmem = pl.BlockSpec(memory_space=pltpu.VMEM)
    dma = pltpu.SemaphoreType.DMA
    wide = pl.pallas_call(
        functools.partial(resample_kernel, sec_count, tile_count),
        out_shape=jax.ShapeDtypeStruct((channels, wide_rows, width), bf16),
        in_specs=[pl.BlockSpec(memory_space=pltpu.HBM)] * (2 + len(tables)),
        out_specs=vmem,
        scratch_shapes=[pltpu.VMEM((bands, ms_rows, ms_cols), bf16)]
        + [pltpu.VMEM(table.shape, table.dtype) for table in tables]
        + [
            pltpu.VMEM((rows + 2 * HALO, cols + 2 * LANES), bf16),
            pltpu.VMEM((2, bands // 2, 16, ms_cols), bf16),
            pltpu.VMEM((2, bands // 2, 16, ms_cols), bf16),
            pltpu.VMEM((2, rows * HALO // LANES, LANES), bf16),
            pltpu.VMEM((2, rows * HALO // LANES, LANES), bf16),
            pltpu.VMEM((2, ms_rows, LANES), bf16),
            pltpu.VMEM((2, ms_rows + 32, LANES), bf16),
            pltpu.VMEM((rows, 2 * LANES), bf16),
            pltpu.VMEM((rows, 2 * LANES), bf16),
            pltpu.VMEM((wide_rows, 2 * LANES), bf16),
            pltpu.VMEM((wide_rows, 2 * LANES), bf16),
            dma,
            dma((len(tables) + 1,)),
        ]
        + [dma((len(STEPS),))] * 6
        + [dma((2 * channels,))] * 2,
        compiler_params=pltpu.CompilerParams(collective_id=0, has_side_effects=True),
    )(pan_source.reshape(rows, cols), ms_source.reshape(bands, ms_rows, ms_cols), *tables)
    fit_rows = rows + EDGE
    sharpened = pl.pallas_call(
        functools.partial(filter_kernel, sec_count, tile_count),
        grid=(bands,),
        out_shape=jax.ShapeDtypeStruct((bands, rows, cols), bf16),
        in_specs=[
            pl.BlockSpec((1, wide_rows, width), lambda b: (0, 0, 0)),
            pl.BlockSpec((1, wide_rows, width), lambda b: (b + 1, 0, 0)),
        ],
        out_specs=pl.BlockSpec((1, rows, cols), lambda b: (b, 0, 0)),
        scratch_shapes=[
            pltpu.VMEM((width, width), bf16),
            pltpu.VMEM((width, cols), bf16),
            pltpu.VMEM((fit_rows, width), f32),
            pltpu.VMEM((rows, cols), f32),
            pltpu.VMEM((fit_rows, width), f32),
            pltpu.VMEM((fit_rows, width), f32),
            pltpu.VMEM((wide_rows, width), f32),
            pltpu.VMEM((wide_rows, width), f32),
            pltpu.VMEM((fit_rows, width), bf16),
            pltpu.VMEM((fit_rows, width), bf16),
        ],
    )(wide, wide)
    return sharpened[:, None]


def solution(mesh):
    tiles = ("sec", "tile")
    table = P(tiles, None)
    return jax.shard_map(
        functools.partial(local, mesh.shape["sec"], mesh.shape["tile"]),
        mesh=mesh,
        in_specs=(P(tiles, None, None), P(None, tiles, None, None)) + (table,) * 8,
        out_specs=P(None, tiles, None, None),
        check_vma=False,
    )
```

```python
import functools

import jax
import jax.numpy as jnp
from jax import lax
from jax.experimental import pallas as pl
from jax.experimental.pallas import tpu as pltpu
from jax.sharding import PartitionSpec as P

HALO = 32
MHALO = 8
RADIUS = 8
EPSILON = 0.1
GRID_COLS = 4
EDGE = 2 * RADIUS
LANES = 128
MESH = pl.DeviceIdType.MESH

STEPS = ((1, 0), (-1, 0), (0, 1), (0, -1), (1, 1), (1, -1), (-1, 1), (-1, -1))


def cubic_weights(fraction):
    squared = fraction * fraction
    cubed = squared * fraction
    return (
        -0.5 * cubed + squared - 0.5 * fraction,
        1.5 * cubed - 2.5 * squared + 1.0,
        -1.5 * cubed + 2.0 * squared + 0.5 * fraction,
        0.5 * cubed - 0.5 * squared,
    )


def band(taps, fraction, length, shift):
    line = lax.broadcasted_iota(jnp.int32, (length, taps.shape[1]), 0)
    return band_at(line - shift, taps, fraction)


def band_at(position, taps, fraction):
    weights = cubic_weights(fraction)
    distance = position - taps
    matrix = jnp.zeros(position.shape, jnp.float32)
    for offset in range(4):
        matrix = jnp.where(distance == offset, weights[offset], matrix)
    return matrix.astype(jnp.bfloat16)


def picker(shape, shift, low, high):
    source = lax.broadcasted_iota(jnp.int32, shape, 0)
    target = lax.broadcasted_iota(jnp.int32, shape, 1)
    chosen = (target - source == shift) & (source >= low) & (source < high)
    return jnp.where(chosen, 1.0, 0.0).astype(jnp.bfloat16)


def dot(left, right):
    return jnp.dot(left, right, preferred_element_type=jnp.float32)


def dot_t(left, right):
    return lax.dot_general(
        left, right, (((0,), (0,)), ((), ())), preferred_element_type=jnp.float32
    )


def place(sec_count, tile_count):
    total = sec_count * tile_count
    me = lax.axis_index("sec") * tile_count + lax.axis_index("tile")
    return lax.rem(me + 2, total), total


def resample_kernel(
    sec_count,
    tile_count,
    pan,
    ms,
    row_tap,
    row_frac,
    col_tap,
    col_frac,
    ms_row_tap,
    ms_row_frac,
    ms_col_tap,
    ms_col_frac,
    wide,
    ms_own,
    row_tap_here,
    row_frac_here,
    col_tap_here,
    col_frac_here,
    ms_row_tap_here,
    ms_row_frac_here,
    ms_col_tap_here,
    ms_col_frac_here,
    pan_patch,
    ms_vert,
    ms_tall,
    pan_pack,
    pan_got,
    ms_pack,
    ms_got,
    pack_east,
    pack_west,
    got_west,
    got_east,
    local_sem,
    table_sem,
    send_pan,
    recv_pan,
    send_ms,
    recv_ms,
    send_edge,
    recv_edge,
    send_tall,
    recv_tall,
):
    rows, cols = pan.shape
    bands, ms_rows, ms_cols = ms.shape
    channels = bands + 1
    placed, total = place(sec_count, tile_count)
    column = lax.rem(placed, GRID_COLS)
    grid_row = placed // GRID_COLS
    north_ok = grid_row > 0
    south_ok = grid_row < total // GRID_COLS - 1
    west_ok = column > 0
    east_ok = column < GRID_COLS - 1

    def device(down, right):
        there = lax.rem(placed + down * GRID_COLS + right - 2 + 2 * total, total)
        return (there // tile_count, lax.rem(there, tile_count))

    def reaches(down, right):
        ok = True
        if down:
            ok = south_ok if down > 0 else north_ok
        if right:
            side = east_ok if right > 0 else west_ok
            ok = side if ok is True else ok & side
        return ok

    def start_all(steps, copies):
        for (down, right), copy in zip(steps, copies):
            pl.when(reaches(down, right))(copy.start)

    def wait_all(steps, copies):
        for (down, right), copy in zip(steps, copies):
            pl.when(reaches(-down, -right))(copy.wait_recv)
        for (down, right), copy in zip(steps, copies):
            pl.when(reaches(down, right))(copy.wait_send)

    barrier = pltpu.get_barrier_semaphore()
    for down, right in STEPS:

        @pl.when(reaches(down, right))
        def _(down=down, right=right):
            pl.semaphore_signal(
                barrier, inc=1, device_id=device(down, right), device_id_type=MESH
            )

    own = pltpu.make_async_copy(
        pan, pan_patch.at[HALO : HALO + rows, LANES : LANES + cols], local_sem
    )
    fetched = [
        pltpu.make_async_copy(source, target, table_sem.at[index])
        for index, (source, target) in enumerate(
            (
                (row_tap, row_tap_here),
                (row_frac, row_frac_here),
                (col_tap, col_tap_here),
                (col_frac, col_frac_here),
                (ms_row_tap, ms_row_tap_here),
                (ms_row_frac, ms_row_frac_here),
                (ms_col_tap, ms_col_tap_here),
                (ms_col_frac, ms_col_frac_here),
                (ms, ms_own),
            )
        )
    ]
    for copy in fetched:
        copy.start()
    own.start()
    for copy in fetched:
        copy.wait()
    own.wait()
    group = rows // (LANES // HALO)
    ms_slot = LANES // 2
    for side in range(2):
        total_pan = jnp.zeros((group, LANES), jnp.float32)
        first_lane = 0 if side else LANES - HALO
        block = slice(LANES, 2 * LANES) if side else slice(cols, cols + LANES)
        for g in range(LANES // HALO):
            move = picker(
                (LANES, LANES), g * HALO - first_lane, first_lane, first_lane + HALO
            )
            lines = slice(HALO + g * group, HALO + (g + 1) * group)
            total_pan = total_pan + dot(pan_patch[lines, block], move)
        pan_pack[side] = total_pan.astype(jnp.bfloat16)
        total_ms = jnp.zeros((ms_rows, LANES), jnp.float32)
        first_lane = 0 if side else ms_cols - MHALO
        for b in range(bands):
            move = picker(
                (ms_cols, LANES),
                side * ms_slot + b * MHALO - first_lane,
                first_lane,
                first_lane + MHALO,
            )
            total_ms = total_ms + dot(ms_own[b], move)
        ms_pack[side] = total_ms.astype(jnp.bfloat16)
        lines = slice(0, MHALO) if side else slice(ms_rows - MHALO, ms_rows)
        for pair in range(bands // 2):
            both = [ms_own[b].astype(jnp.float32)[lines] for b in (2 * pair, 2 * pair + 1)]
            ms_tall[side, pair] = jnp.concatenate(both, axis=0).astype(jnp.bfloat16)

    tall = 1 + north_ok.astype(jnp.int32) + south_ok.astype(jnp.int32)
    broad = 1 + west_ok.astype(jnp.int32) + east_ok.astype(jnp.int32)
    pl.semaphore_wait(barrier, tall * broad - 1)

    def span(step, size, depth):
        if step > 0:
            return slice(size - depth, size), slice(0, depth)
        if step < 0:
            return slice(0, depth), slice(depth + size, 2 * depth + size)
        return slice(0, size), slice(depth, depth + size)

    steps, copies = [], []
    for index, (down, right) in enumerate(STEPS):
        row_from, row_to = span(down, rows, HALO)
        col_from, col_to = span(right, cols, LANES)
        side = 0 if right > 0 else 1
        if down:
            source, target = pan.at[row_from, col_from], pan_patch.at[row_to, col_to]
        else:
            source, target = pan_pack.at[side], pan_got.at[side]
        steps.append((down, right))
        copies.append(
            pltpu.make_async_remote_copy(
                src_ref=source,
                dst_ref=target,
                send_sem=send_pan.at[index],
                recv_sem=recv_pan.at[index],
                device_id=device(down, right),
                device_id_type=MESH,
            )
        )
        row_from, row_to = span(down, ms_rows, 16)
        if right:
            source, target = ms_pack.at[side, row_from, :], ms_got.at[side, row_to, :]
        else:
            source, target = ms_tall.at[0 if down > 0 else 1], ms_vert.at[0 if down > 0 else 1]
        steps.append((down, right))
        copies.append(
            pltpu.make_async_remote_copy(
                src_ref=source,
                dst_ref=target,
                send_sem=send_ms.at[index],
                recv_sem=recv_ms.at[index],
                device_id=device(down, right),
                device_id_type=MESH,
            )
        )
    start_all(steps, copies)
    row_matrix = band(row_tap_here[...], row_frac_here[...], 2 * HALO + rows, 0)
    col_matrix = band(col_tap_here[...], col_frac_here[...], 2 * LANES + cols, LANES - HALO)
    ms_row_taps = ms_row_tap_here[...]
    ms_row_fracs = ms_row_frac_here[...]
    ms_row_matrix = band(ms_row_taps, ms_row_fracs, 32 + ms_rows, 16 - MHALO)
    line = lax.broadcasted_iota(jnp.int32, (32 + ms_rows, rows), 0)
    below = 16 + ms_rows
    away = -LANES
    first_of_pair = jnp.where(
        line < MHALO, line, jnp.where((line < 16) | (line >= below + MHALO), away, line - MHALO)
    )
    second_of_pair = jnp.where(
        line < MHALO,
        away,
        jnp.where(
            line < below, line - MHALO, jnp.where(line < below + MHALO, away, line - 2 * MHALO)
        ),
    )
    ms_pair_matrices = tuple(
        band_at(position, ms_row_taps, ms_row_fracs)
        for position in (first_of_pair, second_of_pair)
    )
    ms_col_taps = ms_col_tap_here[...]
    ms_col_fracs = ms_col_frac_here[...]
    ms_own_matrix = band(ms_col_taps, ms_col_fracs, ms_cols, -MHALO)
    lane = lax.broadcasted_iota(jnp.int32, (LANES, cols), 0)
    ms_halo_matrix = band_at(
        jnp.where(lane < ms_slot, 0, ms_cols + MHALO) + lax.rem(lane, MHALO),
        ms_col_taps,
        ms_col_fracs,
    )

    wait_all(steps, copies)

    def clear(ok, ref):
        @pl.when(jnp.logical_not(ok))
        def _():
            ref[...] = jnp.zeros(ref.shape, ref.dtype)

    clear(west_ok, pan_got.at[0])
    clear(east_ok, pan_got.at[1])
    for side in range(2):
        first_lane = 0 if side else LANES - HALO
        block = slice(LANES + cols, 2 * LANES + cols) if side else slice(0, LANES)
        for g in range(LANES // HALO):
            move = picker((LANES, LANES), first_lane - g * HALO, g * HALO, (g + 1) * HALO)
            lines = slice(HALO + g * group, HALO + (g + 1) * group)
            pan_patch[lines, block] = dot(pan_got[side], move).astype(jnp.bfloat16)

    clear(north_ok, pan_patch.at[:HALO, :])
    clear(south_ok, pan_patch.at[HALO + rows :, :])
    clear(west_ok, pan_patch.at[:, :LANES])
    clear(east_ok, pan_patch.at[:, LANES + cols :])
    clear(north_ok, ms_vert.at[0])
    clear(south_ok, ms_vert.at[1])
    for side, ok in ((0, west_ok), (1, east_ok)):
        clear(ok, ms_got.at[side])
        clear(north_ok, ms_got.at[side, :16, :])
        clear(south_ok, ms_got.at[side, 16 + ms_rows :, :])

    tall_steps, tall_copies = [], []

    def send_rows(c):
        for index, down in enumerate((1, -1)):
            row_from, row_to = span(down, rows, EDGE)
            tall_steps.append((down, 0))
            tall_copies.append(
                pltpu.make_async_remote_copy(
                    src_ref=wide.at[c, slice(row_from.start + EDGE, row_from.stop + EDGE), :cols],
                    dst_ref=wide.at[c, row_to, :cols],
                    send_sem=send_tall.at[2 * c + index],
                    recv_sem=recv_tall.at[2 * c + index],
                    device_id=device(down, 0),
                    device_id_type=MESH,
                )
            )
        start_all(tall_steps[-2:], tall_copies[-2:])

    segment = dot_t(row_matrix, pan_patch[...]).astype(jnp.bfloat16)
    wide[0, EDGE : EDGE + rows, :cols] = dot(segment, col_matrix).astype(jnp.bfloat16)
    lane = lax.broadcasted_iota(jnp.int32, (rows, LANES), 1)
    halo_segment = dot_t(ms_row_matrix, ms_got[0]) + dot_t(ms_row_matrix, ms_got[1])
    halo_band = lax.rem(lane, ms_slot) // MHALO
    for b in range(bands):
        block = jnp.concatenate([ms_vert[0, b // 2], ms_own[b], ms_vert[1, b // 2]], axis=0)
        segment = dot_t(ms_pair_matrices[b % 2], block).astype(jnp.bfloat16)
        beside = jnp.where(halo_band == b, halo_segment, 0.0).astype(jnp.bfloat16)
        wide[b + 1, EDGE : EDGE + rows, :cols] = (
            dot(segment, ms_own_matrix) + dot(beside, ms_halo_matrix)
        ).astype(jnp.bfloat16)
        send_rows(b)

    lane = lax.broadcasted_iota(jnp.int32, (LANES, 2 * LANES), 0)
    slot = lax.broadcasted_iota(jnp.int32, (LANES, 2 * LANES), 1)
    east_sum = jnp.zeros((rows, 2 * LANES), jnp.float32)
    west_sum = jnp.zeros((rows, 2 * LANES), jnp.float32)
    for c in range(channels):
        pick = slot - c * EDGE
        inside = (pick >= 0) & (pick < EDGE)
        last = jnp.where(inside & (lane - (LANES - EDGE) == pick), 1.0, 0.0).astype(jnp.bfloat16)
        first = jnp.where(inside & (lane == pick), 1.0, 0.0).astype(jnp.bfloat16)
        east_sum = east_sum + dot(wide[c, EDGE : EDGE + rows, cols - LANES : cols], last)
        west_sum = west_sum + dot(wide[c, EDGE : EDGE + rows, :LANES], first)
    pack_east[...] = east_sum.astype(jnp.bfloat16)
    pack_west[...] = west_sum.astype(jnp.bfloat16)

    send_rows(bands)
    side_steps = tuple(step for step in STEPS if step[1])
    copies = []
    for index, (down, right) in enumerate(side_steps):
        row_from, row_to = span(down, rows, EDGE)
        if right > 0:
            source, target = pack_east.at[row_from, :], got_west.at[row_to, :]
        else:
            source, target = pack_west.at[row_from, :], got_east.at[row_to, :]
        copies.append(
            pltpu.make_async_remote_copy(
                src_ref=source,
                dst_ref=target,
                send_sem=send_edge.at[index],
                recv_sem=recv_edge.at[index],
                device_id=device(down, right),
                device_id_type=MESH,
            )
        )
    start_all(side_steps, copies)
    wait_all(tuple(tall_steps) + side_steps, tall_copies + copies)

    clear(north_ok, wide.at[:, :EDGE, :cols])
    clear(south_ok, wide.at[:, EDGE + rows :, :cols])
    for got, ok in ((got_west, west_ok), (got_east, east_ok)):
        clear(ok, got)
        clear(north_ok, got.at[:EDGE, :])
        clear(south_ok, got.at[EDGE + rows :, :])
    source = lax.broadcasted_iota(jnp.int32, (2 * LANES, LANES), 0)
    lane = lax.broadcasted_iota(jnp.int32, (2 * LANES, LANES), 1)
    for c in range(channels):
        pick = source - c * EDGE
        inside = (pick >= 0) & (pick < EDGE)
        from_east = jnp.where(inside & (lane == pick), 1.0, 0.0).astype(jnp.bfloat16)
        from_west = jnp.where(inside & (lane - (LANES - EDGE) == pick), 1.0, 0.0).astype(
            jnp.bfloat16
        )
        wide[c, :, cols:] = (
            dot(got_east[...], from_east) + dot(got_west[...], from_west)
        ).astype(jnp.bfloat16)


def sum_down(lines, pairs, fours, kept):
    count = kept + EDGE
    pairs[:count] = lines[:count] + lines[1 : count + 1]
    fours[:count] = pairs[:count] + pairs[2 : count + 2]
    eights = fours[: kept + 8] + fours[4 : kept + 12]
    return eights[:kept] + eights[8:] + lines[EDGE:count]


def store_chunks(target, values):
    for t in range(values.shape[1] // LANES):
        target[t, : values.shape[0]] = values[:, t * LANES : (t + 1) * LANES]


def inverse_cover(first, shape, axis, extent, kept):
    line = lax.broadcasted_iota(jnp.int32, shape, axis)
    places = line + first
    highest = jnp.minimum(places + RADIUS, extent - 1)
    lowest = jnp.maximum(places - RADIUS, 0)
    inside = (places >= 0) & (places < extent) & (line < kept)
    cover = jnp.where(inside, highest - lowest + 1, 1).astype(jnp.float32)
    return jnp.where(inside, 1.0 / cover, 0.0)


def filter_kernel(
    sec_count,
    tile_count,
    guide,
    bandref,
    out,
    box_a,
    box_b,
    inverse,
    inverse_out,
    mean_guide,
    inverse_var,
    sums_a,
    sums_b,
    fit_a,
    fit_b,
    pairs,
    fours,
):
    wide_rows, width = guide.shape[1:]
    rows, cols = out.shape[1:]
    fit_rows = rows + EDGE
    chunks = width // LANES

    def box_across(values, matrix):
        high = values.astype(jnp.bfloat16)
        low = (values - high.astype(jnp.float32)).astype(jnp.bfloat16)
        return dot(high, matrix) + dot(low, matrix)

    @pl.when(pl.program_id(0) == 0)
    def _():
        placed, total = place(sec_count, tile_count)
        column = lax.rem(placed, GRID_COLS)
        grid_row = placed // GRID_COLS
        map_rows = total // GRID_COLS * rows
        map_cols = GRID_COLS * cols
        k = lax.broadcasted_iota(jnp.int32, (width, width), 0)
        j = lax.broadcasted_iota(jnp.int32, (width, width), 1)
        back = j - k
        back = jnp.where(back < 0, back + width, back)
        box_a[...] = jnp.where(back <= EDGE, 1.0, 0.0).astype(jnp.bfloat16)
        k = lax.broadcasted_iota(jnp.int32, (width, cols), 0)
        j = lax.broadcasted_iota(jnp.int32, (width, cols), 1)
        box_b[...] = jnp.where((k >= j) & (k - j <= EDGE), 1.0, 0.0).astype(jnp.bfloat16)
        row0 = grid_row * rows
        col0 = column * cols
        inverse[...] = inverse_cover(
            row0 - RADIUS, (fit_rows, width), 0, map_rows, fit_rows
        ) * inverse_cover(col0 - RADIUS, (fit_rows, width), 1, map_cols, cols + EDGE)
        inverse_out[...] = inverse_cover(row0, (rows, cols), 0, map_rows, rows) * inverse_cover(
            col0, (rows, cols), 1, map_cols, cols
        )
        own = guide[0].astype(jnp.float32)
        store_chunks(sums_a, dot(guide[0], box_a[...]))
        store_chunks(sums_b, box_across(own * own, box_a[...]))
        for t in range(chunks):
            lanes = slice(t * LANES, (t + 1) * LANES)
            scale = inverse[:, lanes]
            mean = sum_down(sums_a.at[t], pairs.at[2 * t + 0], fours.at[2 * t + 0], fit_rows) * scale
            square = sum_down(sums_b.at[t], pairs.at[2 * t + 1], fours.at[2 * t + 1], fit_rows) * scale
            mean_guide[:, lanes] = mean
            inverse_var[:, lanes] = 1.0 / (square - mean * mean + EPSILON)

    store_chunks(sums_a, dot(bandref[0], box_a[...]))
    product = guide[0].astype(jnp.float32) * bandref[0].astype(jnp.float32)
    store_chunks(sums_b, box_across(product, box_a[...]))
    for t in range(chunks):
        lanes = slice(t * LANES, (t + 1) * LANES)
        scale = inverse[:, lanes]
        mean = mean_guide[:, lanes]
        mean_band = sum_down(sums_a.at[t], pairs.at[2 * t + 0], fours.at[2 * t + 0], fit_rows) * scale
        cross = sum_down(sums_b.at[t], pairs.at[2 * t + 1], fours.at[2 * t + 1], fit_rows) * scale
        gain = (cross - mean * mean_band) * inverse_var[:, lanes]
        fit_a[:, lanes] = gain.astype(jnp.bfloat16)
        fit_b[:, lanes] = (mean_band - gain * mean).astype(jnp.bfloat16)
    store_chunks(sums_a, dot(fit_a[...], box_b[...]))
    store_chunks(sums_b, dot(fit_b[...], box_b[...]))
    for t in range(cols // LANES):
        lanes = slice(t * LANES, (t + 1) * LANES)
        own = guide[0, EDGE : EDGE + rows, lanes].astype(jnp.float32)
        gain = sum_down(sums_a.at[t], pairs.at[2 * t + 0], fours.at[2 * t + 0], rows)
        offset = sum_down(sums_b.at[t], pairs.at[2 * t + 1], fours.at[2 * t + 1], rows)
        out[0, :, lanes] = ((gain * own + offset) * inverse_out[:, lanes]).astype(jnp.bfloat16)


def local(sec_count, tile_count, pan_source, ms_source, *tables):
    rows, cols = pan_source.shape[1:]
    bands, _, ms_rows, ms_cols = ms_source.shape
    channels = bands + 1
    wide_rows = rows + 2 * EDGE
    width = cols + LANES
    bf16, f32 = jnp.bfloat16, jnp.float32
    vmem = pl.BlockSpec(memory_space=pltpu.VMEM)
    dma = pltpu.SemaphoreType.DMA
    wide = pl.pallas_call(
        functools.partial(resample_kernel, sec_count, tile_count),
        out_shape=jax.ShapeDtypeStruct((channels, wide_rows, width), bf16),
        in_specs=[pl.BlockSpec(memory_space=pltpu.HBM)] * (2 + len(tables)),
        out_specs=vmem,
        scratch_shapes=[pltpu.VMEM((bands, ms_rows, ms_cols), bf16)]
        + [pltpu.VMEM(table.shape, table.dtype) for table in tables]
        + [
            pltpu.VMEM((rows + 2 * HALO, cols + 2 * LANES), bf16),
            pltpu.VMEM((2, bands // 2, 16, ms_cols), bf16),
            pltpu.VMEM((2, bands // 2, 16, ms_cols), bf16),
            pltpu.VMEM((2, rows * HALO // LANES, LANES), bf16),
            pltpu.VMEM((2, rows * HALO // LANES, LANES), bf16),
            pltpu.VMEM((2, ms_rows, LANES), bf16),
            pltpu.VMEM((2, ms_rows + 32, LANES), bf16),
            pltpu.VMEM((rows, 2 * LANES), bf16),
            pltpu.VMEM((rows, 2 * LANES), bf16),
            pltpu.VMEM((wide_rows, 2 * LANES), bf16),
            pltpu.VMEM((wide_rows, 2 * LANES), bf16),
            dma,
            dma((len(tables) + 1,)),
        ]
        + [dma((len(STEPS),))] * 6
        + [dma((2 * channels,))] * 2,
        compiler_params=pltpu.CompilerParams(collective_id=0, has_side_effects=True),
    )(pan_source.reshape(rows, cols), ms_source.reshape(bands, ms_rows, ms_cols), *tables)
    fit_rows = rows + EDGE
    sharpened = pl.pallas_call(
        functools.partial(filter_kernel, sec_count, tile_count),
        grid=(bands,),
        out_shape=jax.ShapeDtypeStruct((bands, rows, cols), bf16),
        in_specs=[
            pl.BlockSpec((1, wide_rows, width), lambda b: (0, 0, 0)),
            pl.BlockSpec((1, wide_rows, width), lambda b: (b + 1, 0, 0)),
        ],
        out_specs=pl.BlockSpec((1, rows, cols), lambda b: (b, 0, 0)),
        scratch_shapes=[
            pltpu.VMEM((width, width), bf16),
            pltpu.VMEM((width, cols), bf16),
            pltpu.VMEM((fit_rows, width), f32),
            pltpu.VMEM((rows, cols), f32),
            pltpu.VMEM((fit_rows, width), f32),
            pltpu.VMEM((fit_rows, width), f32),
            pltpu.VMEM((width // LANES, wide_rows + EDGE, LANES), f32),
            pltpu.VMEM((width // LANES, wide_rows + EDGE, LANES), f32),
            pltpu.VMEM((fit_rows, width), bf16),
            pltpu.VMEM((fit_rows, width), bf16),
            pltpu.VMEM((2 * width // LANES, wide_rows + EDGE, LANES), f32),
            pltpu.VMEM((2 * width // LANES, wide_rows + EDGE, LANES), f32),
        ],
    )(wide, wide)
    return sharpened[:, None]


def solution(mesh):
    tiles = ("sec", "tile")
    table = P(tiles, None)
    return jax.shard_map(
        functools.partial(local, mesh.shape["sec"], mesh.shape["tile"]),
        mesh=mesh,
        in_specs=(P(tiles, None, None), P(None, tiles, None, None)) + (table,) * 8,
        out_specs=P(None, tiles, None, None),
        check_vma=False,
    )
```
